128 devices in a mesh: macro: 16 (over z, y), pool: 8 (over x, core).
Axes of the slice: x: 4, y: 4, z: 4, core: 2. Of those that a mesh axis runs over, the one named last changes fastest.
Arguments:
- history: float32 [729, 65536], P(None, ('macro', 'pool')), may hold values from -6 to 6
- yield_flags: int32 [729, 65536], P(None, ('macro', 'pool')), may hold values 0 or 1
- strain: float32 [6, 65536], P(None, ('macro', 'pool')), may hold values from -6 to 6
- qp_to_rve: int32 [128, 512], P(('macro', 'pool')), may hold values from 0 to 511, each once within a row
- new_owner: int32 [65536, 1], P(('macro', 'pool')), may hold values from 0 to 127; in each aligned block of 512 rows (0 to 511, 512 to 1023, ...) at most 8 rows name the same one
- stiffness: float32 [9, 9, 81, 81], replicated, as said below
- pattern: int32 [9, 9], replicated, may hold values from 0 to 1, as said below
- coupling: float32 [3, 6, 729], replicated, as said below
- plastic_dir: float32 [3, 729], replicated, may hold values from -6 to 6
Outputs:
- new_history: float32 [729, 131072], P(None, ('macro', 'pool'))
- stress: float32 [6, 65536], P(None, ('macro', 'pool'))
The draws below stay inside these ranges and needn't reach their ends.
Inputs may be any that keep to these rules, and one draw needn't show every extreme that they name: `new_owner`: among the rows of one device no owner is named more than 8 times, a bound that some block reaches. `qp_to_rve`: each row is a permutation of 0 to 511. `pattern`: Symmetric, with ones on the diagonal. stiffness[a, b] is the transpose of stiffness[b, a]; diagonal entries of diagonal blocks lie in 0.5 to 1.5, all others in 0 to 0.032. `coupling`: entries lie in -5.7 to 6.3.
All inputs are finite; a program needn't handle non-finite values. No bound on the sum of `yield_flags` on one device may be relied on, other than what follows from the above.
Results may differ from the reference program's by a relative error of at most 0.0003.
Values sent between devices are 32-bit elements; how exact they have to be, the bound alone decides.
A program may use at most 128 MiB of HBM per device.

```python
import math
import jax
import jax.numpy as jnp
import numpy as np
from jax import lax

NB = 9
BLK = 81
COMP = 3
VOIGT = 6
ITERS = 3
R_DEV = 512
NODES = 729
RVES = 65536
CAP = 8
N_MACRO = 16
N_POOL = 8


def draw_stiffness(key, part):
    key_off = jax.random.fold_in(key, 11)
    key_diag = jax.random.fold_in(key, 12)
    raw = jax.random.uniform(key_off, (NB, NB, BLK, BLK), jnp.float32, 0.0, 0.032)
    sym = 0.5 * (raw + jnp.transpose(raw, (1, 0, 3, 2)))
    diag_vals = jax.random.uniform(key_diag, (NB, BLK), jnp.float32, 0.5, 1.5)
    eye_blocks = (jnp.arange(NB)[:, None] == jnp.arange(NB)[None, :]).astype(jnp.float32)
    eye_nodes = (jnp.arange(BLK)[:, None] == jnp.arange(BLK)[None, :]).astype(jnp.float32)
    on_diag = eye_blocks[:, :, None, None] * eye_nodes[None, None, :, :]
    return sym * (1.0 - on_diag) + diag_vals[:, None, :, None] * on_diag


def draw_pattern(key, part):
    groups = jax.random.randint(jax.random.fold_in(key, 21), (NB,), 0, 3).astype(jnp.int32)
    return (groups[:, None] == groups[None, :]).astype(jnp.int32)


def draw_coupling(key, part):
    key_noise = jax.random.fold_in(key, 31)
    noise = jnp.clip(jax.random.normal(key_noise, (COMP, VOIGT, NODES), jnp.float32), -6.0, 6.0)
    offset = 0.3
    return noise + offset


def set_ends(values, own_key, smallest, high):
    extent = values.shape
    place = [jax.random.randint(jax.random.fold_in(own_key, axis), (), 0, extent[axis]) for axis in range(len(extent))]
    values = values.at[tuple(place)].set(smallest)
    longest = extent.index(max(extent))
    place[longest] = (place[longest] + 1) % extent[longest]
    return values.at[tuple(place)].set(high)


def block_levels(rng, shape, shards, low, high):
    def one(dim, parts):
        heights = jax.random.uniform(jax.random.fold_in(jax.random.fold_in(rng, 6), dim), (parts,), jnp.float32, low / len(shards), high / len(shards))
        return jnp.repeat(jnp.exp(heights), shape[dim] // parts).reshape((-1,) + (1,) * (len(shape) - dim - 1))

    loudness = one(*shards[0])
    for cut in shards[1:]:
        loudness = loudness * one(*cut)
    return loudness


def routed_block(stream_key, own, number, rows, amount, top, bound, lean):
    sequence = jax.random.permutation(stream_key, amount)
    packed, common = shares(amount, rows * top, bound, lean, True), shares(amount, rows * top, bound, lean, False)
    places = jnp.arange(amount)

    def named(tallies, rotation):
        used = int((tallies > 0).sum())
        fixed = max(1, used // 4)
        passed = fixed + (places - fixed + rotation * (used - fixed)) % max(1, amount - fixed)
        return jnp.zeros((amount,), jnp.int32).at[sequence[jnp.where(places < fixed, places, passed)]].set(jnp.asarray(tallies, jnp.int32))

    tallies = jnp.where(number % 4 == 0, named(packed, number // 4), named(common, number - number // 4 - 1))
    mixed = jax.random.permutation(jax.random.fold_in(own, 3), amount)
    giver, receiver = mixed[0:amount // 2 * 2:2], mixed[1:amount // 2 * 2:2]
    room = jnp.minimum(tallies[giver] - 1, bound - tallies[receiver]) // 2
    room = jnp.where((giver == sequence[0]) | (receiver == sequence[0]) | (tallies[receiver] == 0), 0, jnp.maximum(room, 0))
    passed = jax.random.randint(jax.random.fold_in(own, 4), (amount // 2,), 0, 1 << 20) % (room + 1)
    tallies = tallies.at[giver].add(-passed).at[receiver].add(passed)
    items = jnp.searchsorted(jnp.cumsum(tallies), jnp.arange(rows * top), side="right").astype(jnp.int32)
    grid = items.reshape(top, rows).T
    grid = grid[jax.random.permutation(jax.random.fold_in(own, 1), rows)]
    rotation = jax.random.randint(jax.random.fold_in(own, 2), (rows, 1), 0, top)
    return jnp.take_along_axis(grid, (jnp.arange(top)[None, :] + rotation) % top, axis=1)


def shares(number_of, total, limit, skew, full):
    portions = [(1 << 20) // math.isqrt(rank ** skew) + 1 for rank in range(1, number_of + 1)]
    largest = limit if full else min(limit, max(-(-total // number_of), total * portions[0] // sum(portions)))
    least = 1 if total - largest >= number_of - 1 else 0
    holding, rest = [largest] + [least] * (number_of - 1), total - largest - least * (number_of - 1)
    while rest > 0:
        free = [i for i in range(1, number_of) if holding[i] < largest] or [i for i in range(1, number_of) if holding[i] < limit]
        whole, budget = sum([portions[i] for i in free]), rest
        for i in free:
            extra = min(limit - holding[i], max(1, budget * portions[i] // whole), rest)
            holding[i] = holding[i] + extra
            rest = rest - extra
    return np.array(holding)


def bell_draw(own_key, extent, deviation, limit, cuts=(), kind=jnp.bfloat16):
    values = jax.random.normal(own_key, extent, jnp.float32) * deviation
    if len(cuts) > 0:
        values = block_levels(own_key, extent, cuts, -0.22, 0.18) * values
    return jnp.clip(values, min=-limit, max=limit).astype(kind)


def setup_inputs(seed: int = 0) -> dict:
    seeds = jax.random.split(jax.random.key(seed), 10)
    history = bell_draw(seeds[0], (NODES, RVES), 1.0, 6.0, ((1, 128),), jnp.float32)
    yield_flags = set_ends((jax.random.randint(seeds[1], (NODES, RVES), 0, 3) < 1).astype(jnp.int32), jax.random.fold_in(seeds[1], 1), 0, 1)
    strain = bell_draw(seeds[2], (VOIGT, RVES), 1.0, 6.0, ((1, 128),), jnp.float32)
    qp_to_rve = jax.vmap(lambda own: jax.random.permutation(own, R_DEV))(jax.random.split(seeds[3], (N_MACRO * N_POOL))).reshape((N_MACRO * N_POOL, R_DEV)).astype(jnp.int32)
    new_owner_keys = jax.random.split(jax.random.fold_in(seeds[4], 1), RVES // R_DEV)
    new_owner_turns = jax.random.permutation(jax.random.fold_in(seeds[4], 3), RVES // R_DEV)
    new_owner = jax.vmap(lambda own, number: routed_block(jax.random.fold_in(seeds[4], 2), own, number, R_DEV, N_MACRO * N_POOL, 1, CAP, 2))(new_owner_keys, new_owner_turns).reshape((RVES, 1))
    stiffness = draw_stiffness(jax.random.fold_in(seeds[9], 71), 0)
    pattern = draw_pattern(jax.random.fold_in(seeds[9], 71), 0)
    coupling = draw_coupling(jax.random.fold_in(seeds[9], 71), 0)
    plastic_dir = bell_draw(seeds[8], (COMP, NODES), 1.0, 6.0, (), jnp.float32)
    return {"history": history, "yield_flags": yield_flags, "strain": strain, "qp_to_rve": qp_to_rve, "new_owner": new_owner, "stiffness": stiffness, "pattern": pattern, "coupling": coupling, "plastic_dir": plastic_dir}


exact_setting = lax.Precision.HIGHEST

def dense_stiffness(stiffness, pattern):
    block_rows = stiffness.shape[0]
    block_size = stiffness.shape[2]
    masked = stiffness * pattern.astype(jnp.float32)[:, :, None, None]
    return jnp.transpose(masked, (0, 2, 1, 3)).reshape(block_rows * block_size, block_rows * block_size)

def micro_solve(dense_k, coupling, plastic_dir, hist, weight, strain_columns):
    node_total = hist.shape[0]
    component_total = coupling.shape[0]
    columns = hist.shape[1]
    tangent_matrix = 1.5 - weight
    driving = jnp.einsum('ckn,ks->ncs', coupling, strain_columns, precision=exact_setting)
    source = driving - (weight * hist)[:, None, :] * jnp.transpose(plastic_dir)[:, :, None]

    def apply_op(vector_in):
        product = jnp.dot(dense_k, vector_in.reshape(node_total, component_total * columns), precision=exact_setting, preferred_element_type=jnp.float32)
        return product.reshape(node_total, component_total, columns) + tangent_matrix[:, None, :] * vector_in
    solved_field = jnp.zeros_like(source)
    residual = source
    direction = source
    norm_now = lax.optimization_barrier(jnp.sum(residual * residual, axis=(0, 1)))
    for iteration in range(ITERS):
        applied = apply_op(direction)
        step_size = norm_now / jnp.maximum(lax.optimization_barrier(jnp.sum(direction * applied, axis=(0, 1))), 1.0)
        solved_field = solved_field + step_size * direction
        residual = residual - step_size * applied
        norm_next = lax.optimization_barrier(jnp.sum(residual * residual, axis=(0, 1)))
        direction = residual + norm_next / jnp.maximum(norm_now, 1.0) * direction
        norm_now = norm_next
    homogenizing_scale = 1.0 / math.sqrt(component_total * node_total)
    stress_columns = strain_columns + homogenizing_scale * jnp.einsum('dlj,jdf->lf', coupling, tangent_matrix[:, None, :] * solved_field, precision=exact_setting)
    updated = hist + weight * jnp.einsum('cn,ncs->ns', plastic_dir, solved_field, precision=exact_setting)
    return (updated, stress_columns)

def reference(history, yield_flags, strain, qp_to_rve, new_owner, stiffness, pattern, coupling, plastic_dir):
    devices = N_MACRO * N_POOL
    dense_k = dense_stiffness(stiffness, pattern)
    hist_blocks = history.reshape(NODES, devices, R_DEV).transpose(1, 0, 2)
    flag_blocks = yield_flags.reshape(NODES, devices, R_DEV).transpose(1, 0, 2)
    strain_blocks = strain.reshape(VOIGT, devices, R_DEV).transpose(1, 0, 2)
    owner_blocks = new_owner.reshape(devices, R_DEV).astype(jnp.int32)

    def one_block(pieces):
        hist, flags, strain_part, qmap, owner = pieces
        weight = flags.astype(jnp.float32) * hist * hist / (1.0 + hist * hist)
        rve_strain = jnp.zeros_like(strain_part).at[:, qmap.astype(jnp.int32)].set(strain_part)
        updated, stress_rve = micro_solve(dense_k, coupling, plastic_dir, hist, weight, rve_strain)
        stress_qp = stress_rve[:, qmap.astype(jnp.int32)]
        onehot = (owner[:, None] == jnp.arange(devices, dtype=jnp.int32)[None, :]).astype(jnp.int32)
        rank = lax.optimization_barrier(jnp.sum((jnp.cumsum(onehot, axis=0) - onehot) * onehot, axis=1)).astype(jnp.int32)
        return (updated, stress_qp, rank)
    updated, stress_qp, rank = lax.map(one_block, (hist_blocks, flag_blocks, strain_blocks, qp_to_rve, owner_blocks))
    sources = jnp.arange(devices, dtype=jnp.int32)[:, None]
    column = (owner_blocks * (devices * CAP) + sources * CAP + rank).astype(jnp.int32)
    values = updated.transpose(1, 0, 2).reshape(NODES, devices * R_DEV)
    new_history = jnp.zeros((NODES, devices * devices * CAP), jnp.float32).at[:, column.reshape(-1)].set(values)
    stress_out = stress_qp.transpose(1, 0, 2).reshape(VOIGT, devices * R_DEV)
    return (new_history, stress_out)
```

```python
import functools
import math

import jax
import jax.numpy as jnp
from jax import lax
from jax.experimental import pallas as pl
from jax.experimental.pallas import tpu as pltpu
from jax.sharding import PartitionSpec as P

ITERS = 3
NB = 9
BLK = 81
COMP = 3
VOIGT = 6
NODES = NB * BLK
NP = 768
RV = 512
BW = 128
NBLK = RV // BW
DEV = 128
CAP = 8
CH = 64
STRIDE = 53
LOG = pl.DeviceIdType.LOGICAL
F32 = jnp.float32
BF = jnp.bfloat16


def split2(x):
    hi = x.astype(BF)
    return hi, (x - hi.astype(F32)).astype(BF)


def split3(x):
    hi = x.astype(BF)
    rest = x - hi.astype(F32)
    mid = rest.astype(BF)
    return hi, mid, (rest - mid.astype(F32)).astype(BF)


def dot(a, b):
    return jnp.dot(a, b, preferred_element_type=F32)


def to_columns(row):
    return jnp.transpose(jnp.broadcast_to(row, (BW, RV)))


def iota(shape, dim):
    return lax.broadcasted_iota(jnp.int32, shape, dim).astype(F32)


def kernel(
    hist_hbm, flag_hbm, strain_hbm, qp_hbm, owner_hbm, stiff_hbm, pat_ref, coup_hbm, plast_hbm,
    out_ref, stress_ref,
    hist_v, flag_v, strain_v, qp_v, owner_v, stiff_v, coup_v, plast_v,
    k32, kk, hcat, fcat, pos, slot, qcol, slotrow, s24, ct, gmat, pb,
    w_s, h_s, x_s, r_s, d_s, im_s, dd, ycat, ucat, stress_acc, ship, recv,
    in_sem, loc_sem, send_sem, recv_sem,
):
    me = lax.axis_index("macro") * 8 + lax.axis_index("pool")
    pairs = (
        (owner_hbm, owner_v), (qp_hbm, qp_v), (stiff_hbm, stiff_v), (hist_hbm, hist_v),
        (flag_hbm, flag_v), (strain_hbm, strain_v), (coup_hbm, coup_v), (plast_hbm, plast_v),
    )
    loads = [pltpu.make_async_copy(a, b, in_sem.at[i]) for i, (a, b) in enumerate(pairs)]
    for load in loads:
        load.start()

    barrier = pltpu.get_barrier_semaphore()

    def greet(i, carry):
        pl.semaphore_signal(barrier, inc=1, device_id=lax.rem(me + i, DEV), device_id_type=LOG)
        return carry

    lax.fori_loop(1, DEV, greet, 0)

    loads[0].wait()
    loads[1].wait()
    owner_row = owner_v[...].astype(F32)
    owner_col = to_columns(owner_row)
    qcol[...] = to_columns(qp_v[...].astype(F32))
    e_col = iota((RV, BW), 0)
    rank_part = jnp.zeros((RV, BW), F32)
    rank_rows = []
    for t in range(NBLK):
        e_row = iota((RV, BW), 1) + float(t * BW)
        same = owner_col == owner_row[:, t * BW : (t + 1) * BW]
        rank_part += jnp.where(same & (e_row < e_col), 1.0, 0.0)
        rank_rows.append(
            jnp.sum(jnp.where(same & (e_col < e_row), 1.0, 0.0), axis=0, keepdims=True)
        )
    rank_col = jnp.broadcast_to(jnp.sum(rank_part, axis=1, keepdims=True), (RV, BW))
    key_col = rank_col * float(RV) - e_col
    pos_part = jnp.zeros((RV, BW), F32)
    for t in range(NBLK):
        key_row = rank_rows[t] * float(RV) - (iota((1, BW), 1) + float(t * BW))
        pos_part += jnp.where(key_row > key_col, 1.0, 0.0)
    pos[...] = jnp.broadcast_to(jnp.sum(pos_part, axis=1, keepdims=True), (RV, BW))
    slot[...] = owner_col * float(CAP) + rank_col
    slotrow[...] = jnp.full(slotrow.shape, -1.0, F32)

    k32[...] = jnp.zeros_like(k32)
    loads[2].wait()
    for a in range(NB):
        row = [stiff_v[a, b] * pat_ref[a, b].astype(F32) for b in range(NB)]
        k32[pl.ds(a * BLK, BLK), pl.ds(0, NODES)] = jnp.concatenate(row, axis=1)

    def split_k(i, carry):
        rows = pl.ds(pl.multiple_of(i * CH, CH), CH)
        hi, lo = split2(k32[rows, :])
        kk[rows, pl.ds(0, NP)] = hi
        kk[rows, pl.ds(NP, NP)] = hi
        kk[rows, pl.ds(2 * NP, NP)] = lo
        return carry

    lax.fori_loop(0, NP // CH, split_k, 0)

    loads[3].wait()
    loads[4].wait()
    hcat[pl.ds(NP - 64, 64), :] = jnp.zeros((64, 2 * RV), BF)
    fcat[pl.ds(NP - 64, 64), :] = jnp.zeros((64, RV), BF)

    def split_h(i, carry):
        rows = pl.ds(pl.multiple_of(i * CH, CH), CH)
        hi, lo = split2(hist_v[rows, :])
        hcat[rows, pl.ds(0, RV)] = hi
        hcat[rows, pl.ds(RV, RV)] = lo
        fcat[rows, :] = flag_v[rows, :].astype(F32).astype(BF)
        return carry

    whole = NODES // CH
    lax.fori_loop(0, whole, split_h, 0)
    rest = pl.ds(whole * CH, NODES - whole * CH)
    hi, lo = split2(hist_v[rest, :])
    hcat[rest, pl.ds(0, RV)] = hi
    hcat[rest, pl.ds(RV, RV)] = lo
    fcat[rest, :] = flag_v[rest, :].astype(F32).astype(BF)

    for i in range(5, 8):
        loads[i].wait()
    two = jnp.zeros((2, RV), F32)
    s24[...] = jnp.concatenate(
        [p.astype(F32) for p in split3(jnp.concatenate([strain_v[...], two], axis=0))], axis=0
    ).astype(BF)
    edge = jnp.zeros((2, NODES), F32)
    coup = [jnp.concatenate([coup_v[c], edge], axis=0) for c in range(COMP)]
    pad = jnp.zeros((CAP, NP - NODES), F32)
    coup = [jnp.concatenate([c, pad], axis=1) for c in coup]
    chi = [c.astype(BF).astype(F32) for c in coup]
    clo = [c - h for c, h in zip(coup, chi)]
    ct[...] = jnp.transpose(
        jnp.concatenate(chi + clo + chi + [jnp.zeros((BW - 72, NP), F32)], axis=0)
    ).astype(BF)
    for c in range(COMP):
        gmat[:, pl.ds(c * NP, NP)] = jnp.concatenate([chi[c], clo[c]], axis=0).astype(BF)
        line = jnp.concatenate([plast_v[pl.ds(c, 1), :], pad[0:1]], axis=1)
        pb[c] = jnp.transpose(jnp.broadcast_to(line, (BW, NP)))
    stress_acc[...] = jnp.zeros_like(stress_acc)
    ucat[...] = jnp.zeros_like(ucat)

    def chunks(body, init):
        def step(i, carry):
            return body(pl.ds(pl.multiple_of(i * CH, CH), CH), i, carry)

        return lax.fori_loop(0, NP // CH, step, init)

    def fold(v):
        return jnp.sum(v.reshape(CH // 8, 8, BW), axis=0)

    zero8 = jnp.zeros((8, BW), F32)

    def block(b, carry):
        lane = iota((1, BW), 1) + (b * BW).astype(F32)
        chosen = pos[...] == lane
        e_row = jnp.sum(jnp.where(chosen, iota((RV, BW), 0), 0.0), axis=0, keepdims=True)
        s_row = jnp.sum(jnp.where(chosen, slot[...], 0.0), axis=0, keepdims=True)
        slotrow[:, pl.ds(pl.multiple_of(b * BW, BW), BW)] = jnp.broadcast_to(s_row, (8, BW))
        perm = jnp.where(chosen, 1.0, 0.0).astype(BF)
        serves = jnp.where(qcol[...] == e_row, 1.0, 0.0).astype(BF)
        h_s[...] = dot(hcat[...], jnp.concatenate([perm, perm], axis=0))
        w_s[...] = dot(fcat[...], perm)
        parts = dot(s24[...], serves)
        strain = parts[0:8] + parts[8:16] + parts[16:24]
        sh = strain.astype(BF).astype(F32)
        sl = strain - sh
        cols = []
        for c in range(COMP):
            rows = [zero8] * (BW // 8)
            rows[c], rows[3 + c], rows[6 + c] = sh, sh, sl
            cols.append(jnp.concatenate(rows, axis=0))
        drive = jnp.concatenate(cols, axis=1).astype(BF)
        im_s[...] = dot(ct[...], drive)

        def source(rows, i, rr):
            h = h_s[rows, :]
            h2 = h * h
            w = w_s[rows, :] * h2 / (1.0 + h2)
            w_s[rows, :] = w
            wh = w * h
            for c in range(COMP):
                lanes = pl.ds(c * BW, BW)
                v = im_s[rows, lanes] - wh * pb[c, rows, :]
                x_s[rows, lanes] = jnp.zeros((CH, BW), F32)
                r_s[rows, lanes] = v
                d_s[rows, lanes] = v
                hi, lo = split2(v)
                dd[pl.ds(pl.multiple_of(i * CH, CH), CH), lanes] = hi
                dd[pl.ds(pl.multiple_of(NP + i * CH, CH), CH), lanes] = lo
                dd[pl.ds(pl.multiple_of(2 * NP + i * CH, CH), CH), lanes] = hi
                rr = rr + fold(v * v)
            return rr

        rr0 = jnp.sum(chunks(source, zero8), axis=0, keepdims=True)

        def iterate(it, rr):
            im_s[...] = dot(kk[...], dd[...])

            def apply(rows, i, acc):
                tan = 1.5 - w_s[rows, :]
                for c in range(COMP):
                    lanes = pl.ds(c * BW, BW)
                    d = d_s[rows, lanes]
                    im = im_s[rows, lanes] + tan * d
                    im_s[rows, lanes] = im
                    acc = acc + fold(d * im)
                return acc

            energy = jnp.sum(chunks(apply, zero8), axis=0, keepdims=True)
            size = rr / jnp.maximum(energy, 1.0)

            def advance(rows, i, acc):
                for c in range(COMP):
                    lanes = pl.ds(c * BW, BW)
                    x_s[rows, lanes] = x_s[rows, lanes] + size * d_s[rows, lanes]
                    r = r_s[rows, lanes] - size * im_s[rows, lanes]
                    r_s[rows, lanes] = r
                    acc = acc + fold(r * r)
                return acc

            after = jnp.sum(chunks(advance, zero8), axis=0, keepdims=True)
            ratio = after / jnp.maximum(rr, 1.0)

            def turn(rows, i, acc):
                for c in range(COMP):
                    lanes = pl.ds(c * BW, BW)
                    d = r_s[rows, lanes] + ratio * d_s[rows, lanes]
                    d_s[rows, lanes] = d
                    hi, lo = split2(d)
                    dd[pl.ds(pl.multiple_of(i * CH, CH), CH), lanes] = hi
                    dd[pl.ds(pl.multiple_of(NP + i * CH, CH), CH), lanes] = lo
                    dd[pl.ds(pl.multiple_of(2 * NP + i * CH, CH), CH), lanes] = hi
                return acc

            @pl.when(it < ITERS - 1)
            def _():
                chunks(turn, 0)

            return after

        lax.fori_loop(0, ITERS, iterate, rr0)

        def finish(rows, i, acc):
            w = w_s[rows, :]
            tan = 1.5 - w
            flow = jnp.zeros((CH, BW), F32)
            for c in range(COMP):
                x = x_s[rows, pl.ds(c * BW, BW)]
                flow = flow + pb[c, rows, :] * x
                hi, lo = split2(tan * x)
                there = pl.ds(pl.multiple_of(c * NP + i * CH, CH), CH)
                ycat[there, pl.ds(0, BW)] = hi
                ycat[there, pl.ds(BW, BW)] = lo
            h_s[rows, :] = h_s[rows, :] + w * flow
            return acc

        chunks(finish, 0)

        hi, lo = split2(jnp.transpose(h_s[...]))
        ucat[pl.ds(pl.multiple_of(b * BW, BW), BW), :] = hi
        ucat[pl.ds(pl.multiple_of(RV + b * BW, BW), BW), :] = lo
        first = 2.0 * (NBLK - 1 - b).astype(F32)
        t8 = float(CAP) * iota((DEV, RV), 0) + first
        srow = slotrow[0:1, :]
        place = jnp.concatenate(
            [jnp.where(srow == t8, 1.0, 0.0), jnp.where(srow == t8 + 1.0, 1.0, 0.0)], axis=0
        ).astype(BF)
        moved = dot(jnp.concatenate([place, place], axis=1), ucat[...])

        for k in range(NBLK):
            j = NBLK - 1 - k

            @pl.when(b == k)
            def _():
                ship[:, 2 * j, :] = moved[0:DEV]
                ship[:, 2 * j + 1, :] = moved[DEV:]
                if k == 0:
                    pl.semaphore_wait(barrier, DEV - 1)

                def send(i, c):
                    peer = lax.rem(me + i * STRIDE, DEV)
                    pltpu.make_async_remote_copy(
                        src_ref=ship.at[peer, pl.ds(2 * j, 2)],
                        dst_ref=recv.at[me, pl.ds(2 * j, 2)],
                        send_sem=send_sem.at[k],
                        recv_sem=recv_sem.at[k],
                        device_id=peer,
                        device_id_type=LOG,
                    ).start()
                    return c

                lax.fori_loop(1, DEV, send, 0)

        both = dot(gmat[...], ycat[...])
        delta = both[0:8, 0:BW] + both[8:16, 0:BW] + both[0:8, BW : 2 * BW]
        stress = strain + delta * (1.0 / math.sqrt(COMP * NODES))
        st24 = jnp.concatenate([p.astype(F32) for p in split3(stress)], axis=0).astype(BF)
        back = lax.dot_general(
            st24, serves, (((1,), (1,)), ((), ())), preferred_element_type=F32
        )
        stress_acc[...] += back[0:8] + back[8:16] + back[16:24]
        return carry

    lax.fori_loop(0, NBLK, block, 0)
    own = pltpu.make_async_copy(ship.at[me], recv.at[me], loc_sem)
    own.start()
    stress_ref[...] = stress_acc[0:VOIGT, :]
    own.wait()
    for k in range(NBLK):
        two_rows = pl.ds(2 * (NBLK - 1 - k), 2)
        some = pl.ds(0, DEV - 1)
        pltpu.make_async_copy(ship.at[some, two_rows], recv.at[some, two_rows], recv_sem.at[k]).wait()
        pltpu.make_async_copy(ship.at[some, two_rows], recv.at[some, two_rows], send_sem.at[k]).wait()

    def turn_out(i, carry):
        piece = recv[pl.ds(pl.multiple_of(i * 16, 16), 16)].reshape(BW, NP)
        out_ref[:, pl.ds(pl.multiple_of(i * BW, BW), BW)] = jnp.transpose(piece)[0:NODES]
        return carry

    lax.fori_loop(0, DEV // 16, turn_out, 0)


def shards(
    history, yield_flags, strain, qp_to_rve, new_owner, stiffness, pattern, coupling, plastic_dir
):
    owner = new_owner.reshape(1, RV)
    hbm = pl.BlockSpec(memory_space=pl.ANY)
    vmem = pl.BlockSpec(memory_space=pltpu.VMEM)
    v = pltpu.VMEM
    return pl.pallas_call(
        kernel,
        out_shape=(
            jax.ShapeDtypeStruct((NODES, DEV * CAP), F32),
            jax.ShapeDtypeStruct((VOIGT, RV), F32),
        ),
        in_specs=[hbm] * 6 + [pl.BlockSpec(memory_space=pltpu.SMEM)] + [hbm] * 2,
        out_specs=(vmem, vmem),
        scratch_shapes=[
            v((NODES, RV), F32), v((NODES, RV), jnp.int32), v((VOIGT, RV), F32),
            v((1, RV), jnp.int32), v((1, RV), jnp.int32), v((NB, NB, BLK, BLK), F32),
            v((COMP, VOIGT, NODES), F32), v((COMP, NODES), F32),
            v((NP, NP), F32), v((NP, 3 * NP), BF), v((NP, 2 * RV), BF), v((NP, RV), BF),
            v((RV, BW), F32), v((RV, BW), F32), v((RV, BW), F32), v((8, RV), F32),
            v((24, RV), BF), v((NP, BW), BF), v((16, COMP * NP), BF), v((COMP, NP, BW), F32),
            v((NP, BW), F32), v((NP, BW), F32), v((NP, COMP * BW), F32), v((NP, COMP * BW), F32),
            v((NP, COMP * BW), F32), v((NP, COMP * BW), F32), v((3 * NP, COMP * BW), BF),
            v((COMP * NP, 2 * BW), BF), v((2 * RV, NP), BF), v((8, RV), F32),
            v((DEV, CAP, NP), F32), v((DEV, CAP, NP), F32),
            pltpu.SemaphoreType.DMA((8,)), pltpu.SemaphoreType.DMA(()),
            pltpu.SemaphoreType.DMA((NBLK,)), pltpu.SemaphoreType.DMA((NBLK,)),
        ],
        compiler_params=pltpu.CompilerParams(
            collective_id=0, has_side_effects=True, vmem_limit_bytes=56 * 1024 * 1024
        ),
        name="micro_newton",
    )(
        history, yield_flags, strain, qp_to_rve, owner, stiffness, pattern, coupling, plastic_dir
    )


def solution(mesh):
    both = ("macro", "pool")
    return jax.shard_map(
        shards,
        mesh=mesh,
        in_specs=(
            P(None, both), P(None, both), P(None, both), P(both, None), P(both, None),
            P(), P(), P(), P(),
        ),
        out_specs=(P(None, both), P(None, both)),
        check_vma=False,
    )
```

```python
import functools
import math

import jax
import jax.numpy as jnp
from jax import lax
from jax.experimental import pallas as pl
from jax.experimental.pallas import tpu as pltpu
from jax.sharding import PartitionSpec as P

ITERS = 3
NB = 9
BLK = 81
COMP = 3
VOIGT = 6
NODES = NB * BLK
NP = 768
RV = 512
BW = 128
NBLK = RV // BW
DEV = 128
CAP = 8
CH = 64
RC = 8
UNROLL = 16
STRIDE = 53
LOG = pl.DeviceIdType.LOGICAL
F32 = jnp.float32
BF = jnp.bfloat16


def split2(x):
    hi = x.astype(BF)
    return hi, (x - hi.astype(F32)).astype(BF)


def split3(x):
    hi = x.astype(BF)
    rest = x - hi.astype(F32)
    mid = rest.astype(BF)
    return hi, mid, (rest - mid.astype(F32)).astype(BF)


def dot(a, b):
    return jnp.dot(a, b, preferred_element_type=F32)


def to_columns(row):
    return jnp.transpose(jnp.broadcast_to(row, (BW, RV)))


def iota(shape, dim):
    return lax.broadcasted_iota(jnp.int32, shape, dim).astype(F32)


def dot_t(a, b):
    return lax.dot_general(a, b, (((1,), (1,)), ((), ())), preferred_element_type=F32)


def stack(parts):
    return jnp.concatenate([p.astype(F32) for p in parts], axis=0).astype(BF)


def kernel(
    hist_hbm, flag_hbm, strain_hbm, qp_hbm, owner_hbm, stiff_hbm, pat_ref, coup_hbm, plast_hbm,
    out_ref, stress_ref,
    hist_v, flag_v, strain_v, qp_v, owner_v, stiff_v, coup_v, plast_v,
    k32, kk, hcat, fcat, slotrow, s32, permt, servest, drive, prow, gmat,
    h_s, w_s, r0_s, r1_s, r2_s, im0_s, y_s, dd, ycat, ucat, coef, ship, recv,
    in_sem, loc_sem, send_sem, recv_sem,
):
    me = lax.axis_index("macro") * 8 + lax.axis_index("pool")
    pairs = (
        (owner_hbm, owner_v), (qp_hbm, qp_v), (stiff_hbm, stiff_v), (hist_hbm, hist_v),
        (flag_hbm, flag_v), (strain_hbm, strain_v), (coup_hbm, coup_v), (plast_hbm, plast_v),
    )
    loads = [pltpu.make_async_copy(a, b, in_sem.at[i]) for i, (a, b) in enumerate(pairs)]
    for load in loads:
        load.start()

    barrier = pltpu.get_barrier_semaphore()

    def greet(i, carry):
        pl.semaphore_signal(barrier, inc=1, device_id=lax.rem(me + i, DEV), device_id_type=LOG)
        return carry

    lax.fori_loop(1, DEV, greet, 0)

    loads[0].wait()
    loads[1].wait()
    owner_row = owner_v[...].astype(F32)
    owner_col = to_columns(owner_row)
    qp_row = qp_v[...].astype(F32)
    e_col = iota((RV, BW), 0)
    rank_part = jnp.zeros((RV, BW), F32)
    rank_rows = []
    for t in range(NBLK):
        e_row = iota((RV, BW), 1) + float(t * BW)
        same = owner_col == owner_row[:, t * BW : (t + 1) * BW]
        rank_part += jnp.where(same & (e_row < e_col), 1.0, 0.0)
        rank_rows.append(
            jnp.sum(jnp.where(same & (e_col < e_row), 1.0, 0.0), axis=0, keepdims=True)
        )
    rank_col = jnp.broadcast_to(jnp.sum(rank_part, axis=1, keepdims=True), (RV, BW))
    key_col = rank_col * float(RV) - e_col
    e_part = jnp.zeros((RV, BW), F32)
    slot_part = jnp.zeros((RV, BW), F32)
    for t in range(NBLK):
        lanes = pl.ds(t * BW, BW)
        e_row = iota((1, BW), 1) + float(t * BW)
        key_row = rank_rows[t] * float(RV) - e_row
        pos_row = jnp.sum(jnp.where(key_col > key_row, 1.0, 0.0), axis=0, keepdims=True)
        slot_row = owner_row[:, t * BW : (t + 1) * BW] * float(CAP) + rank_rows[t]
        chosen = iota((RV, BW), 0) == pos_row
        e_part += jnp.where(chosen, e_row, 0.0)
        slot_part += jnp.where(chosen, slot_row, 0.0)
        one = jnp.where(chosen, 1.0, 0.0).astype(BF)
        permt[:, lanes] = one
        permt[:, pl.ds(RV + t * BW, BW)] = one
    e_of = jnp.broadcast_to(jnp.sum(e_part, axis=1, keepdims=True), (RV, BW))
    slot_of = jnp.broadcast_to(jnp.sum(slot_part, axis=1, keepdims=True), (RV, BW))
    slotrow[...] = jnp.transpose(slot_of)[0:8]
    for t in range(NBLK):
        lanes = pl.ds(t * BW, BW)
        hit = e_of == qp_row[:, t * BW : (t + 1) * BW]
        servest[:, lanes] = jnp.where(hit, 1.0, 0.0).astype(BF)

    for i in range(5, 8):
        loads[i].wait()
    shi, smid, slo = split3(jnp.concatenate([strain_v[...], jnp.zeros((2, RV), F32)], axis=0))
    s32[...] = stack([shi, shi, smid, slo])
    strain_t = dot_t(servest[...], s32[...]).astype(BF)
    edge = jnp.zeros((2, NODES), F32)
    pad = jnp.zeros((CAP, NP - NODES), F32)
    cols = []
    for c in range(COMP):
        coup = jnp.concatenate([jnp.concatenate([coup_v[c], edge], axis=0), pad], axis=1)
        chi = coup.astype(BF).astype(F32)
        clo = coup - chi
        gmat[:, pl.ds(c * NP, NP)] = jnp.concatenate([chi, clo], axis=0).astype(BF)
        cols.append(jnp.concatenate([chi, clo, chi, jnp.zeros((8, NP), F32)], axis=0))
        line = jnp.concatenate([plast_v[pl.ds(c, 1), :], pad[0:1]], axis=1)
        prow[c] = jnp.broadcast_to(line, (8, NP))
    drive[...] = dot(strain_t, jnp.concatenate(cols, axis=1).astype(BF))

    loads[3].wait()
    loads[4].wait()
    hcat[pl.ds(NP - 64, 64), :] = jnp.zeros((64, 2 * RV), BF)
    fcat[pl.ds(NP - 64, 64), :] = jnp.zeros((64, RV), BF)

    def split_h(i, carry):
        rows = pl.ds(pl.multiple_of(i * CH, CH), CH)
        hi, lo = split2(hist_v[rows, :])
        hcat[rows, pl.ds(0, RV)] = hi
        hcat[rows, pl.ds(RV, RV)] = lo
        fcat[rows, :] = flag_v[rows, :].astype(F32).astype(BF)
        return carry

    whole = NODES // CH
    lax.fori_loop(0, whole, split_h, 0)
    rest = pl.ds(whole * CH, NODES - whole * CH)
    hi, lo = split2(hist_v[rest, :])
    hcat[rest, pl.ds(0, RV)] = hi
    hcat[rest, pl.ds(RV, RV)] = lo
    fcat[rest, :] = flag_v[rest, :].astype(F32).astype(BF)
    h_s[...] = dot_t(permt[...], hcat[...])
    w_s[...] = dot_t(permt[:, 0:RV], fcat[...])

    k32[...] = jnp.zeros_like(k32)
    loads[2].wait()
    for a in range(NB):
        row = [stiff_v[a, b] * pat_ref[a, b].astype(F32) for b in range(NB)]
        k32[pl.ds(a * BLK, BLK), pl.ds(0, NODES)] = jnp.concatenate(row, axis=1)

    def split_k(i, carry):
        hi, lo = split2(k32[pl.ds(pl.multiple_of(i * CH, CH), CH), :])
        kk[pl.ds(pl.multiple_of(i * CH, CH), CH), :] = hi
        kk[pl.ds(pl.multiple_of(NP + i * CH, CH), CH), :] = lo
        kk[pl.ds(pl.multiple_of(2 * NP + i * CH, CH), CH), :] = hi
        return carry

    lax.fori_loop(0, NP // CH, split_k, 0)
    ucat[...] = jnp.zeros_like(ucat)

    def chunks(body):
        def step(i, carry):
            body(i)
            return carry

        lax.fori_loop(0, BW // RC, step, 0, unroll=UNROLL)

    def at(base, i):
        return pl.ds(pl.multiple_of(base + i * RC, RC), RC)

    def total(acc):
        part = acc[:, 0:128]
        for k in range(1, NP // 128):
            part = part + acc[:, k * 128 : (k + 1) * 128]
        return jnp.sum(part, axis=1, keepdims=True)

    def keep(k, i, col):
        coef[k, at(0, i), :] = jnp.broadcast_to(col, (RC, 128))

    def kept(k, i):
        return coef[k, at(0, i), 0:1]

    def put(rows, v, low=True):
        hi = v.astype(BF).astype(F32)
        dd[rows, pl.ds(0, NP)] = hi
        if low:
            dd[rows, pl.ds(NP, NP)] = v - hi

    def block(b, carry):
        base = b * BW

        def source(i):
            here = at(base, i)
            h = h_s[here, :]
            h2 = h * h
            w = w_s[here, :] * h2 / (1.0 + h2)
            w_s[here, :] = w
            wh = w * h
            acc = jnp.zeros((RC, NP), F32)
            for c in range(COMP):
                rows = at(c * BW, i)
                v = drive[here, pl.ds(c * NP, NP)] - wh * prow[c, 0:RC, :]
                r0_s[rows, :] = v
                put(rows, v)
                acc = acc + v * v
            keep(0, i, total(acc))

        chunks(source)

        def product(parts):
            left = dd[...].astype(BF)
            hi = left[:, 0:NP]
            cat = [hi, hi] + ([left[:, NP:]] if parts == 3 else [])
            return dot(jnp.concatenate(cat, axis=1), kk[0 : parts * NP, :])

        im0_s[...] = product(3)

        def first(i):
            tan = 1.5 - w_s[at(base, i), :]
            acc = jnp.zeros((RC, NP), F32)
            ims = []
            for c in range(COMP):
                rows = at(c * BW, i)
                r = r0_s[rows, :]
                im = im0_s[rows, :] + tan * r
                im0_s[rows, :] = im
                ims.append(im)
                acc = acc + r * im
            rr = kept(0, i)
            size = rr / jnp.maximum(total(acc), 1.0)
            acc = jnp.zeros((RC, NP), F32)
            for c in range(COMP):
                rows = at(c * BW, i)
                r = r0_s[rows, :] - size * ims[c]
                r1_s[rows, :] = r
                put(rows, r)
                acc = acc + r * r
            after = total(acc)
            keep(1, i, size)
            keep(2, i, after)
            keep(3, i, after / jnp.maximum(rr, 1.0))

        chunks(first)
        y_s[...] = product(3)

        def second(i):
            tan = 1.5 - w_s[at(base, i), :]
            ratio = kept(3, i)
            acc = jnp.zeros((RC, NP), F32)
            ims = []
            for c in range(COMP):
                rows = at(c * BW, i)
                r = r1_s[rows, :]
                im = y_s[rows, :] + tan * r + ratio * im0_s[rows, :]
                ims.append(im)
                acc = acc + (r + ratio * r0_s[rows, :]) * im
            rr = kept(2, i)
            energy = total(acc)
            size = rr / jnp.maximum(energy, 1.0)
            sq = jnp.zeros((RC, NP), F32)
            cross = jnp.zeros((RC, NP), F32)
            for c in range(COMP):
                rows = at(c * BW, i)
                r = r1_s[rows, :] - size * ims[c]
                r2_s[rows, :] = r
                put(rows, r, low=False)
                sq = sq + r * r
                cross = cross + r * ims[c]
            after = total(sq)
            ratio = after / jnp.maximum(rr, 1.0)
            keep(4, i, size)
            keep(5, i, after)
            keep(6, i, ratio)
            keep(7, i, total(tan * sq) + ratio * (2.0 * total(cross) + ratio * energy))

        chunks(second)
        y_s[...] = product(2)

        def last(i):
            here = at(base, i)
            w = w_s[here, :]
            tan = 1.5 - w
            acc = jnp.zeros((RC, NP), F32)
            for c in range(COMP):
                rows = at(c * BW, i)
                r = r2_s[rows, :]
                acc = acc + (2.0 * r - dd[rows, pl.ds(0, NP)]) * y_s[rows, :]
            a2 = kept(5, i) / jnp.maximum(total(acc) + kept(7, i), 1.0)
            a1 = kept(4, i) + a2 * kept(6, i)
            a0 = kept(1, i) + a1 * kept(3, i)
            flow = jnp.zeros((RC, NP), F32)
            for c in range(COMP):
                rows = at(c * BW, i)
                x = a0 * r0_s[rows, :] + a1 * r1_s[rows, :] + a2 * r2_s[rows, :]
                flow = flow + prow[c, 0:RC, :] * x
                ycat[here, pl.ds(c * NP, NP)] = tan * x
            h_s[here, :] = h_s[here, :] + w * flow

        chunks(last)

        hi, lo = split2(h_s[pl.ds(pl.multiple_of(base, BW), BW), :])
        ucat[pl.ds(pl.multiple_of(base, BW), BW), :] = hi
        ucat[pl.ds(pl.multiple_of(RV + base, BW), BW), :] = lo
        first_slot = 2.0 * (NBLK - 1 - b).astype(F32)
        t8 = float(CAP) * iota((DEV, RV), 0) + first_slot
        srow = jnp.where(iota((1, RV), 1) < ((b + 1) * BW).astype(F32), slotrow[0:1, :], -1.0)
        place = jnp.concatenate(
            [jnp.where(srow == t8, 1.0, 0.0), jnp.where(srow == t8 + 1.0, 1.0, 0.0)], axis=0
        ).astype(BF)
        moved = dot(jnp.concatenate([place, place], axis=1), ucat[...])

        for k in range(NBLK):
            j = NBLK - 1 - k

            @pl.when(b == k)
            def _():
                ship[:, 2 * j, :] = moved[0:DEV]
                ship[:, 2 * j + 1, :] = moved[DEV:]
                if k == 0:
                    pl.semaphore_wait(barrier, DEV - 1)

                def send(i, c):
                    peer = lax.rem(me + i * STRIDE, DEV)
                    pltpu.make_async_remote_copy(
                        src_ref=ship.at[peer, pl.ds(2 * j, 2)],
                        dst_ref=recv.at[me, pl.ds(2 * j, 2)],
                        send_sem=send_sem.at[k],
                        recv_sem=recv_sem.at[k],
                        device_id=peer,
                        device_id_type=LOG,
                    ).start()
                    return c

                lax.fori_loop(1, DEV, send, 0, unroll=16)

        return carry

    lax.fori_loop(0, NBLK, block, 0)
    own = pltpu.make_async_copy(ship.at[me], recv.at[me], loc_sem)
    own.start()

    strain_p = dot_t(s32[...], servest[...])
    delta = jnp.zeros((8, RV), F32)
    for c in range(COMP):
        lanes = pl.ds(c * NP, NP)
        hi, lo = split2(ycat[:, lanes])
        with_hi = dot_t(gmat[:, lanes], hi)
        delta += with_hi[0:8] + with_hi[8:16] + dot_t(gmat[:, lanes], lo)[0:8]
    stress = strain_p[8:16] + strain_p[16:24] + strain_p[24:32]
    stress = stress + delta * (1.0 / math.sqrt(COMP * NODES))
    back = dot(stack(split3(stress)), servest[...])
    stress_ref[...] = (back[0:8] + back[8:16] + back[16:24])[0:VOIGT]
    own.wait()
    for k in range(NBLK):
        two_rows = pl.ds(2 * (NBLK - 1 - k), 2)
        some = pl.ds(0, DEV - 1)
        pltpu.make_async_copy(ship.at[some, two_rows], recv.at[some, two_rows], recv_sem.at[k]).wait()
        pltpu.make_async_copy(ship.at[some, two_rows], recv.at[some, two_rows], send_sem.at[k]).wait()

    def turn_out(i, carry):
        piece = recv[pl.ds(pl.multiple_of(i * 16, 16), 16)].reshape(BW, NP)
        out_ref[:, pl.ds(pl.multiple_of(i * BW, BW), BW)] = jnp.transpose(piece)[0:NODES]
        return carry

    lax.fori_loop(0, DEV // 16, turn_out, 0)


def shards(
    history, yield_flags, strain, qp_to_rve, new_owner, stiffness, pattern, coupling, plastic_dir
):
    owner = new_owner.reshape(1, RV)
    hbm = pl.BlockSpec(memory_space=pl.ANY)
    vmem = pl.BlockSpec(memory_space=pltpu.VMEM)
    v = pltpu.VMEM
    return pl.pallas_call(
        kernel,
        out_shape=(
            jax.ShapeDtypeStruct((NODES, DEV * CAP), F32),
            jax.ShapeDtypeStruct((VOIGT, RV), F32),
        ),
        in_specs=[hbm] * 6 + [pl.BlockSpec(memory_space=pltpu.SMEM)] + [hbm] * 2,
        out_specs=(vmem, vmem),
        scratch_shapes=[
            v((NODES, RV), F32), v((NODES, RV), jnp.int32), v((VOIGT, RV), F32),
            v((1, RV), jnp.int32), v((1, RV), jnp.int32), v((NB, NB, BLK, BLK), F32),
            v((COMP, VOIGT, NODES), F32), v((COMP, NODES), F32),
            v((NP, NP), F32), v((3 * NP, NP), BF), v((NP, 2 * RV), BF), v((NP, RV), BF),
            v((8, RV), F32), v((32, RV), BF), v((RV, 2 * RV), BF), v((RV, RV), BF),
            v((RV, COMP * NP), F32), v((COMP, 8, NP), F32), v((16, COMP * NP), BF),
            v((RV, NP), F32), v((RV, NP), F32),
            v((COMP * BW, NP), F32), v((COMP * BW, NP), F32), v((COMP * BW, NP), F32),
            v((COMP * BW, NP), F32), v((COMP * BW, NP), F32), v((COMP * BW, 2 * NP), F32),
            v((RV, COMP * NP), F32), v((2 * RV, NP), BF), v((8, BW, 128), F32),
            v((DEV, CAP, NP), F32), v((DEV, CAP, NP), F32),
            pltpu.SemaphoreType.DMA((8,)), pltpu.SemaphoreType.DMA(()),
            pltpu.SemaphoreType.DMA((NBLK,)), pltpu.SemaphoreType.DMA((NBLK,)),
        ],
        compiler_params=pltpu.CompilerParams(
            collective_id=0, has_side_effects=True, vmem_limit_bytes=56 * 1024 * 1024
        ),
        name="micro_newton",
    )(
        history, yield_flags, strain, qp_to_rve, owner, stiffness, pattern, coupling, plastic_dir
    )


def solution(mesh):
    both = ("macro", "pool")
    return jax.shard_map(
        shards,
        mesh=mesh,
        in_specs=(
            P(None, both), P(None, both), P(None, both), P(both, None), P(both, None),
            P(), P(), P(), P(),
        ),
        out_specs=(P(None, both), P(None, both)),
        check_vma=False,
    )
```

```python
import functools
import math

import jax
import jax.numpy as jnp
from jax import lax
from jax.experimental import pallas as pl
from jax.experimental.pallas import tpu as pltpu
from jax.sharding import PartitionSpec as P

ITERS = 3
NB = 9
BLK = 81
COMP = 3
VOIGT = 6
NODES = NB * BLK
NP = 768
RV = 512
BW = 128
NBLK = RV // BW
DEV = 128
CAP = 8
CH = 64
RC = 8
UNROLL = 16
OUTW = 256
STRIDE = 53
LOG = pl.DeviceIdType.LOGICAL
F32 = jnp.float32
BF = jnp.bfloat16


def split2(x):
    hi = x.astype(BF)
    return hi, (x - hi.astype(F32)).astype(BF)


def split3(x):
    hi = x.astype(BF)
    rest = x - hi.astype(F32)
    mid = rest.astype(BF)
    return hi, mid, (rest - mid.astype(F32)).astype(BF)


def dot(a, b):
    return jnp.dot(a, b, preferred_element_type=F32)


def to_columns(row):
    return jnp.transpose(jnp.broadcast_to(row, (BW, RV)))


def iota(shape, dim):
    return lax.broadcasted_iota(jnp.int32, shape, dim).astype(F32)


def dot_t(a, b):
    return lax.dot_general(a, b, (((1,), (1,)), ((), ())), preferred_element_type=F32)


def stack(parts):
    return jnp.concatenate([p.astype(F32) for p in parts], axis=0).astype(BF)


def kernel(
    hist_hbm, flag_hbm, strain_hbm, qp_hbm, owner_hbm, stiff_hbm, pat_ref, coup_hbm, plast_hbm,
    recv, stress_ref,
    hist_v, flag_v, strain_v, qp_v, owner_v, stiff_v, coup_v, plast_v,
    k32, kk, hcat, fcat, slotrow, s32, permt, servest, drive, prow, gmat,
    h_s, w_s, r0_s, r1_s, r2_s, im0_s, y_s, dd, ycat, ucat, coef, ship,
    in_sem, loc_sem, send_sem, recv_sem,
):
    me = lax.axis_index("macro") * 8 + lax.axis_index("pool")
    pairs = (
        (owner_hbm, owner_v), (qp_hbm, qp_v), (stiff_hbm, stiff_v), (hist_hbm, hist_v),
        (flag_hbm, flag_v), (strain_hbm, strain_v), (coup_hbm, coup_v), (plast_hbm, plast_v),
    )
    loads = [pltpu.make_async_copy(a, b, in_sem.at[i]) for i, (a, b) in enumerate(pairs)]
    for load in loads:
        load.start()

    barrier = pltpu.get_barrier_semaphore()

    def greet(i, carry):
        pl.semaphore_signal(barrier, inc=1, device_id=lax.rem(me + i, DEV), device_id_type=LOG)
        return carry

    lax.fori_loop(1, DEV, greet, 0)

    loads[0].wait()
    loads[1].wait()
    owner_row = owner_v[...].astype(F32)
    owner_col = to_columns(owner_row)
    qp_row = qp_v[...].astype(F32)
    e_col = iota((RV, BW), 0)
    rank_part = jnp.zeros((RV, BW), F32)
    rank_rows = []
    for t in range(NBLK):
        e_row = iota((RV, BW), 1) + float(t * BW)
        same = owner_col == owner_row[:, t * BW : (t + 1) * BW]
        rank_part += jnp.where(same & (e_row < e_col), 1.0, 0.0)
        rank_rows.append(
            jnp.sum(jnp.where(same & (e_col < e_row), 1.0, 0.0), axis=0, keepdims=True)
        )
    rank_col = jnp.broadcast_to(jnp.sum(rank_part, axis=1, keepdims=True), (RV, BW))
    key_col = rank_col * float(RV) - e_col
    e_part = jnp.zeros((RV, BW), F32)
    slot_part = jnp.zeros((RV, BW), F32)
    for t in range(NBLK):
        lanes = pl.ds(t * BW, BW)
        e_row = iota((1, BW), 1) + float(t * BW)
        key_row = rank_rows[t] * float(RV) - e_row
        pos_row = jnp.sum(jnp.where(key_col > key_row, 1.0, 0.0), axis=0, keepdims=True)
        slot_row = owner_row[:, t * BW : (t + 1) * BW] * float(CAP) + rank_rows[t]
        chosen = iota((RV, BW), 0) == pos_row
        e_part += jnp.where(chosen, e_row, 0.0)
        slot_part += jnp.where(chosen, slot_row, 0.0)
        one = jnp.where(chosen, 1.0, 0.0).astype(BF)
        permt[:, lanes] = one
        permt[:, pl.ds(RV + t * BW, BW)] = one
    e_of = jnp.broadcast_to(jnp.sum(e_part, axis=1, keepdims=True), (RV, BW))
    slot_of = jnp.broadcast_to(jnp.sum(slot_part, axis=1, keepdims=True), (RV, BW))
    slotrow[...] = jnp.transpose(slot_of)[0:8]
    for t in range(NBLK):
        lanes = pl.ds(t * BW, BW)
        hit = e_of == qp_row[:, t * BW : (t + 1) * BW]
        servest[:, lanes] = jnp.where(hit, 1.0, 0.0).astype(BF)

    for i in range(5, 8):
        loads[i].wait()
    shi, smid, slo = split3(jnp.concatenate([strain_v[...], jnp.zeros((2, RV), F32)], axis=0))
    s32[...] = stack([shi, shi, smid, slo])
    strain_t = dot_t(servest[...], s32[...]).astype(BF)
    edge = jnp.zeros((2, NODES), F32)
    pad = jnp.zeros((CAP, NP - NODES), F32)
    cols = []
    for c in range(COMP):
        coup = jnp.concatenate([jnp.concatenate([coup_v[c], edge], axis=0), pad], axis=1)
        chi = coup.astype(BF).astype(F32)
        clo = coup - chi
        gmat[:, pl.ds(c * NP, NP)] = jnp.concatenate([chi, clo], axis=0).astype(BF)
        cols.append(jnp.concatenate([chi, clo, chi, jnp.zeros((8, NP), F32)], axis=0))
        line = jnp.concatenate([plast_v[pl.ds(c, 1), :], pad[0:1]], axis=1)
        prow[c] = jnp.broadcast_to(line, (8, NP))
    drive[...] = dot(strain_t, jnp.concatenate(cols, axis=1).astype(BF))

    loads[3].wait()
    loads[4].wait()
    hcat[pl.ds(NP - 64, 64), :] = jnp.zeros((64, 2 * RV), BF)
    fcat[pl.ds(NP - 64, 64), :] = jnp.zeros((64, RV), BF)

    def split_h(i, carry):
        rows = pl.ds(pl.multiple_of(i * CH, CH), CH)
        hi, lo = split2(hist_v[rows, :])
        hcat[rows, pl.ds(0, RV)] = hi
        hcat[rows, pl.ds(RV, RV)] = lo
        fcat[rows, :] = flag_v[rows, :].astype(F32).astype(BF)
        return carry

    whole = NODES // CH
    lax.fori_loop(0, whole, split_h, 0)
    rest = pl.ds(whole * CH, NODES - whole * CH)
    hi, lo = split2(hist_v[rest, :])
    hcat[rest, pl.ds(0, RV)] = hi
    hcat[rest, pl.ds(RV, RV)] = lo
    fcat[rest, :] = flag_v[rest, :].astype(F32).astype(BF)
    h_s[...] = dot_t(permt[...], hcat[...])
    w_s[...] = dot_t(permt[:, 0:RV], fcat[...])

    k32[...] = jnp.zeros_like(k32)
    loads[2].wait()
    for a in range(NB):
        row = [stiff_v[a, b] * pat_ref[a, b].astype(F32) for b in range(NB)]
        k32[pl.ds(a * BLK, BLK), pl.ds(0, NODES)] = jnp.concatenate(row, axis=1)

    def split_k(i, carry):
        hi, lo = split2(k32[pl.ds(pl.multiple_of(i * CH, CH), CH), :])
        kk[pl.ds(pl.multiple_of(i * CH, CH), CH), :] = hi
        kk[pl.ds(pl.multiple_of(NP + i * CH, CH), CH), :] = lo
        kk[pl.ds(pl.multiple_of(2 * NP + i * CH, CH), CH), :] = hi
        return carry

    lax.fori_loop(0, NP // CH, split_k, 0)
    ucat[...] = jnp.zeros_like(ucat)

    def chunks(body):
        def step(i, carry):
            body(i)
            return carry

        lax.fori_loop(0, BW // RC, step, 0, unroll=UNROLL)

    def at(base, i):
        return pl.ds(pl.multiple_of(base + i * RC, RC), RC)

    def total(acc):
        part = acc[:, 0:128]
        for k in range(1, NP // 128):
            part = part + acc[:, k * 128 : (k + 1) * 128]
        return jnp.sum(part, axis=1, keepdims=True)

    def keep(k, i, col):
        coef[k, at(0, i), :] = jnp.broadcast_to(col, (RC, 128))

    def kept(k, i):
        return coef[k, at(0, i), 0:1]

    def put(rows, v, low=True):
        hi = v.astype(BF).astype(F32)
        dd[rows, pl.ds(0, NP)] = hi
        if low:
            dd[rows, pl.ds(NP, NP)] = v - hi

    def block(b, carry):
        base = b * BW

        def source(i):
            here = at(base, i)
            h = h_s[here, :]
            h2 = h * h
            w = w_s[here, :] * h2 / (1.0 + h2)
            w_s[here, :] = w
            wh = w * h
            acc = jnp.zeros((RC, NP), F32)
            for c in range(COMP):
                rows = at(c * BW, i)
                v = drive[here, pl.ds(c * NP, NP)] - wh * prow[c, 0:RC, :]
                r0_s[rows, :] = v
                put(rows, v)
                acc = acc + v * v
            keep(0, i, total(acc))

        chunks(source)

        def product(parts):
            left = dd[...].astype(BF)
            hi = left[:, 0:NP]
            cat = [hi, hi] + ([left[:, NP:]] if parts == 3 else [])
            return dot(jnp.concatenate(cat, axis=1), kk[0 : parts * NP, :])

        im0_s[...] = product(3)

        def first(i):
            tan = 1.5 - w_s[at(base, i), :]
            acc = jnp.zeros((RC, NP), F32)
            ims = []
            for c in range(COMP):
                rows = at(c * BW, i)
                r = r0_s[rows, :]
                im = im0_s[rows, :] + tan * r
                im0_s[rows, :] = im
                ims.append(im)
                acc = acc + r * im
            rr = kept(0, i)
            size = rr / jnp.maximum(total(acc), 1.0)
            acc = jnp.zeros((RC, NP), F32)
            for c in range(COMP):
                rows = at(c * BW, i)
                r = r0_s[rows, :] - size * ims[c]
                r1_s[rows, :] = r
                put(rows, r)
                acc = acc + r * r
            after = total(acc)
            keep(1, i, size)
            keep(2, i, after)
            keep(3, i, after / jnp.maximum(rr, 1.0))

        chunks(first)
        y_s[...] = product(3)

        def second(i):
            tan = 1.5 - w_s[at(base, i), :]
            ratio = kept(3, i)
            acc = jnp.zeros((RC, NP), F32)
            ims = []
            for c in range(COMP):
                rows = at(c * BW, i)
                r = r1_s[rows, :]
                im = y_s[rows, :] + tan * r + ratio * im0_s[rows, :]
                ims.append(im)
                acc = acc + (r + ratio * r0_s[rows, :]) * im
            rr = kept(2, i)
            energy = total(acc)
            size = rr / jnp.maximum(energy, 1.0)
            sq = jnp.zeros((RC, NP), F32)
            cross = jnp.zeros((RC, NP), F32)
            for c in range(COMP):
                rows = at(c * BW, i)
                r = r1_s[rows, :] - size * ims[c]
                r2_s[rows, :] = r
                put(rows, r, low=False)
                sq = sq + r * r
                cross = cross + r * ims[c]
            after = total(sq)
            ratio = after / jnp.maximum(rr, 1.0)
            keep(4, i, size)
            keep(5, i, after)
            keep(6, i, ratio)
            keep(7, i, total(tan * sq) + ratio * (2.0 * total(cross) + ratio * energy))

        chunks(second)
        y_s[...] = product(2)

        def last(i):
            here = at(base, i)
            w = w_s[here, :]
            tan = 1.5 - w
            acc = jnp.zeros((RC, NP), F32)
            for c in range(COMP):
                rows = at(c * BW, i)
                r = r2_s[rows, :]
                acc = acc + (2.0 * r - dd[rows, pl.ds(0, NP)]) * y_s[rows, :]
            a2 = kept(5, i) / jnp.maximum(total(acc) + kept(7, i), 1.0)
            a1 = kept(4, i) + a2 * kept(6, i)
            a0 = kept(1, i) + a1 * kept(3, i)
            flow = jnp.zeros((RC, NP), F32)
            for c in range(COMP):
                rows = at(c * BW, i)
                x = a0 * r0_s[rows, :] + a1 * r1_s[rows, :] + a2 * r2_s[rows, :]
                flow = flow + prow[c, 0:RC, :] * x
                ycat[here, pl.ds(c * NP, NP)] = tan * x
            h_s[here, :] = h_s[here, :] + w * flow

        chunks(last)

        hi, lo = split2(h_s[pl.ds(pl.multiple_of(base, BW), BW), :])
        ucat[pl.ds(pl.multiple_of(base, BW), BW), :] = hi
        ucat[pl.ds(pl.multiple_of(RV + base, BW), BW), :] = lo
        first_slot = 2.0 * (NBLK - 1 - b).astype(F32)
        t8 = float(CAP) * iota((DEV, RV), 0) + first_slot
        srow = jnp.where(iota((1, RV), 1) < ((b + 1) * BW).astype(F32), slotrow[0:1, :], -1.0)
        place = jnp.concatenate(
            [jnp.where(srow == t8, 1.0, 0.0), jnp.where(srow == t8 + 1.0, 1.0, 0.0)], axis=0
        ).astype(BF)
        moved = dot(jnp.concatenate([place, place], axis=1), ucat[...])

        for k in range(NBLK):
            j = NBLK - 1 - k

            @pl.when(b == k)
            def _():
                ship[:, 2 * j, :] = moved[0:DEV]
                ship[:, 2 * j + 1, :] = moved[DEV:]
                if k == 0:
                    pl.semaphore_wait(barrier, DEV - 1)

                def send(i, c):
                    peer = lax.rem(me + i * STRIDE, DEV)
                    pltpu.make_async_remote_copy(
                        src_ref=ship.at[peer, pl.ds(2 * j, 2)],
                        dst_ref=recv.at[me, pl.ds(2 * j, 2)],
                        send_sem=send_sem.at[k],
                        recv_sem=recv_sem.at[k],
                        device_id=peer,
                        device_id_type=LOG,
                    ).start()
                    return c

                lax.fori_loop(1, DEV, send, 0, unroll=16)

        return carry

    lax.fori_loop(0, NBLK, block, 0)
    own = pltpu.make_async_copy(ship.at[me], recv.at[me], loc_sem)
    own.start()

    strain_p = dot_t(s32[...], servest[...])
    delta = jnp.zeros((8, RV), F32)
    for c in range(COMP):
        lanes = pl.ds(c * NP, NP)
        hi, lo = split2(ycat[:, lanes])
        with_hi = dot_t(gmat[:, lanes], hi)
        delta += with_hi[0:8] + with_hi[8:16] + dot_t(gmat[:, lanes], lo)[0:8]
    stress = strain_p[8:16] + strain_p[16:24] + strain_p[24:32]
    stress = stress + delta * (1.0 / math.sqrt(COMP * NODES))
    back = dot(stack(split3(stress)), servest[...])
    stress_ref[...] = (back[0:8] + back[8:16] + back[16:24])[0:VOIGT]
    own.wait()
    for k in range(NBLK):
        two_rows = pl.ds(2 * (NBLK - 1 - k), 2)
        some = pl.ds(0, DEV - 1)
        pltpu.make_async_copy(ship.at[some, two_rows], recv.at[some, two_rows], recv_sem.at[k]).wait()
        pltpu.make_async_copy(ship.at[some, two_rows], recv.at[some, two_rows], send_sem.at[k]).wait()


def turn(raw_ref, raw_stress_ref, out_hbm, stress_ref, buf, sem):
    stress_ref[...] = raw_stress_ref[...]
    copies = []
    for i in range(DEV * CAP // OUTW):
        for k in range(OUTW // BW):
            first = i * OUTW + k * BW
            piece = raw_ref[pl.ds(first // CAP, BW // CAP)].reshape(BW, NP)
            buf[:, pl.ds(first, BW)] = jnp.transpose(piece)[0:NODES]
        part = pl.ds(i * OUTW, OUTW)
        copies.append(pltpu.make_async_copy(buf.at[:, part], out_hbm.at[:, part], sem.at[i]))
        copies[i].start()
    for copy in copies:
        copy.wait()


def shards(
    history, yield_flags, strain, qp_to_rve, new_owner, stiffness, pattern, coupling, plastic_dir
):
    owner = new_owner.reshape(1, RV)
    hbm = pl.BlockSpec(memory_space=pl.ANY)
    vmem = pl.BlockSpec(memory_space=pltpu.VMEM)
    v = pltpu.VMEM
    raw, raw_stress = pl.pallas_call(
        kernel,
        out_shape=(
            v((DEV, CAP, NP), F32),
            v((VOIGT, RV), F32),
        ),
        in_specs=[hbm] * 6 + [pl.BlockSpec(memory_space=pltpu.SMEM)] + [hbm] * 2,
        out_specs=(vmem, vmem),
        scratch_shapes=[
            v((NODES, RV), F32), v((NODES, RV), jnp.int32), v((VOIGT, RV), F32),
            v((1, RV), jnp.int32), v((1, RV), jnp.int32), v((NB, NB, BLK, BLK), F32),
            v((COMP, VOIGT, NODES), F32), v((COMP, NODES), F32),
            v((NP, NP), F32), v((3 * NP, NP), BF), v((NP, 2 * RV), BF), v((NP, RV), BF),
            v((8, RV), F32), v((32, RV), BF), v((RV, 2 * RV), BF), v((RV, RV), BF),
            v((RV, COMP * NP), F32), v((COMP, 8, NP), F32), v((16, COMP * NP), BF),
            v((RV, NP), F32), v((RV, NP), F32),
            v((COMP * BW, NP), F32), v((COMP * BW, NP), F32), v((COMP * BW, NP), F32),
            v((COMP * BW, NP), F32), v((COMP * BW, NP), F32), v((COMP * BW, 2 * NP), F32),
            v((RV, COMP * NP), F32), v((2 * RV, NP), BF), v((8, BW, 128), F32),
            v((DEV, CAP, NP), F32),
            pltpu.SemaphoreType.DMA((8,)), pltpu.SemaphoreType.DMA(()),
            pltpu.SemaphoreType.DMA((NBLK,)), pltpu.SemaphoreType.DMA((NBLK,)),
        ],
        compiler_params=pltpu.CompilerParams(
            collective_id=0, has_side_effects=True, vmem_limit_bytes=56 * 1024 * 1024
        ),
        name="micro_newton",
    )(
        history, yield_flags, strain, qp_to_rve, owner, stiffness, pattern, coupling, plastic_dir
    )
    return pl.pallas_call(
        turn,
        out_shape=(
            jax.ShapeDtypeStruct((NODES, DEV * CAP), F32),
            jax.ShapeDtypeStruct((VOIGT, RV), F32),
        ),
        in_specs=[vmem, vmem],
        out_specs=(hbm, vmem),
        scratch_shapes=[
            v((NODES, DEV * CAP), F32), pltpu.SemaphoreType.DMA((DEV * CAP // OUTW,)),
        ],
        compiler_params=pltpu.CompilerParams(vmem_limit_bytes=16 * 1024 * 1024),
        name="turn_history",
    )(raw, raw_stress)


def solution(mesh):
    both = ("macro", "pool")
    return jax.shard_map(
        shards,
        mesh=mesh,
        in_specs=(
            P(None, both), P(None, both), P(None, both), P(both, None), P(both, None),
            P(), P(), P(), P(),
        ),
        out_specs=(P(None, both), P(None, both)),
        check_vma=False,
    )
```

```python
import functools
import math

import jax
import jax.numpy as jnp
from jax import lax
from jax.experimental import pallas as pl
from jax.experimental.pallas import tpu as pltpu
from jax.sharding import PartitionSpec as P

ITERS = 3
NB = 9
BLK = 81
COMP = 3
VOIGT = 6
NODES = NB * BLK
NP = 768
RV = 512
BW = 128
NBLK = RV // BW
DEV = 128
CAP = 8
CH = 64
RC = 8
UNROLL = 16
OUTW = 256
STRIDE = 53
LOG = pl.DeviceIdType.LOGICAL
F32 = jnp.float32
BF = jnp.bfloat16


def split2(x):
    hi = x.astype(BF)
    return hi, (x - hi.astype(F32)).astype(BF)


def split3(x):
    hi = x.astype(BF)
    rest = x - hi.astype(F32)
    mid = rest.astype(BF)
    return hi, mid, (rest - mid.astype(F32)).astype(BF)


def dot(a, b):
    return jnp.dot(a, b, preferred_element_type=F32)


def to_columns(row):
    return jnp.transpose(jnp.broadcast_to(row, (BW, RV)))


def iota(shape, dim):
    return lax.broadcasted_iota(jnp.int32, shape, dim).astype(F32)


def dot_t(a, b):
    return lax.dot_general(a, b, (((1,), (1,)), ((), ())), preferred_element_type=F32)


def stack(parts):
    return jnp.concatenate([p.astype(F32) for p in parts], axis=0).astype(BF)


def kernel(
    hist_hbm, flag_hbm, strain_hbm, qp_hbm, owner_hbm, stiff_hbm, pat_ref, coup_hbm, plast_hbm,
    recv, stress_ref,
    hist_v, flag_v, strain_v, qp_v, owner_v, stiff_v, coup_v, plast_v,
    k32, kk, hcat, fcat, slotrow, s32, permt, servest, drive, prow, gmat,
    h_s, w_s, r0_s, r1_s, r2_s, im0_s, y_s, ycat, ucat, coef, sums, ship,
    in_sem, loc_sem, send_sem, recv_sem,
):
    me = lax.axis_index("macro") * 8 + lax.axis_index("pool")
    pairs = (
        (owner_hbm, owner_v), (qp_hbm, qp_v), (stiff_hbm, stiff_v), (hist_hbm, hist_v),
        (flag_hbm, flag_v), (strain_hbm, strain_v), (coup_hbm, coup_v), (plast_hbm, plast_v),
    )
    loads = [pltpu.make_async_copy(a, b, in_sem.at[i]) for i, (a, b) in enumerate(pairs)]
    for load in loads:
        load.start()

    barrier = pltpu.get_barrier_semaphore()

    def greet(i, carry):
        pl.semaphore_signal(barrier, inc=1, device_id=lax.rem(me + i, DEV), device_id_type=LOG)
        return carry

    lax.fori_loop(1, DEV, greet, 0)

    loads[0].wait()
    loads[1].wait()
    owner_row = owner_v[...].astype(F32)
    owner_col = to_columns(owner_row)
    qp_row = qp_v[...].astype(F32)
    e_col = iota((RV, BW), 0)
    rank_part = jnp.zeros((RV, BW), F32)
    rank_rows = []
    for t in range(NBLK):
        e_row = iota((RV, BW), 1) + float(t * BW)
        same = owner_col == owner_row[:, t * BW : (t + 1) * BW]
        rank_part += jnp.where(same & (e_row < e_col), 1.0, 0.0)
        rank_rows.append(
            jnp.sum(jnp.where(same & (e_col < e_row), 1.0, 0.0), axis=0, keepdims=True)
        )
    rank_col = jnp.broadcast_to(jnp.sum(rank_part, axis=1, keepdims=True), (RV, BW))
    key_col = rank_col * float(RV) - e_col
    e_part = jnp.zeros((RV, BW), F32)
    slot_part = jnp.zeros((RV, BW), F32)
    for t in range(NBLK):
        lanes = pl.ds(t * BW, BW)
        e_row = iota((1, BW), 1) + float(t * BW)
        key_row = rank_rows[t] * float(RV) - e_row
        pos_row = jnp.sum(jnp.where(key_col > key_row, 1.0, 0.0), axis=0, keepdims=True)
        slot_row = owner_row[:, t * BW : (t + 1) * BW] * float(CAP) + rank_rows[t]
        chosen = iota((RV, BW), 0) == pos_row
        e_part += jnp.where(chosen, e_row, 0.0)
        slot_part += jnp.where(chosen, slot_row, 0.0)
        one = jnp.where(chosen, 1.0, 0.0).astype(BF)
        permt[:, lanes] = one
        permt[:, pl.ds(RV + t * BW, BW)] = one
    e_of = jnp.broadcast_to(jnp.sum(e_part, axis=1, keepdims=True), (RV, BW))
    slot_of = jnp.broadcast_to(jnp.sum(slot_part, axis=1, keepdims=True), (RV, BW))
    slotrow[...] = jnp.transpose(slot_of)[0:8]
    for t in range(NBLK):
        lanes = pl.ds(t * BW, BW)
        hit = e_of == qp_row[:, t * BW : (t + 1) * BW]
        servest[:, lanes] = jnp.where(hit, 1.0, 0.0).astype(BF)

    for i in range(5, 8):
        loads[i].wait()
    shi, smid, slo = split3(jnp.concatenate([strain_v[...], jnp.zeros((2, RV), F32)], axis=0))
    s32[...] = stack([shi, shi, smid, slo])
    strain_t = dot_t(servest[...], s32[...]).astype(BF)
    edge = jnp.zeros((2, NODES), F32)
    pad = jnp.zeros((CAP, NP - NODES), F32)
    cols = []
    for c in range(COMP):
        coup = jnp.concatenate([jnp.concatenate([coup_v[c], edge], axis=0), pad], axis=1)
        chi = coup.astype(BF).astype(F32)
        clo = coup - chi
        gmat[:, pl.ds(c * NP, NP)] = jnp.concatenate([chi, clo], axis=0).astype(BF)
        cols.append(jnp.concatenate([chi, clo, chi, jnp.zeros((8, NP), F32)], axis=0))
        line = jnp.concatenate([plast_v[pl.ds(c, 1), :], pad[0:1]], axis=1)
        prow[c] = jnp.broadcast_to(line, (8, NP))
    drive[...] = dot(strain_t, jnp.concatenate(cols, axis=1).astype(BF))

    loads[3].wait()
    loads[4].wait()
    hcat[pl.ds(NP - 64, 64), :] = jnp.zeros((64, 2 * RV), BF)
    fcat[pl.ds(NP - 64, 64), :] = jnp.zeros((64, RV), BF)

    def split_h(i, carry):
        rows = pl.ds(pl.multiple_of(i * CH, CH), CH)
        hi, lo = split2(hist_v[rows, :])
        hcat[rows, pl.ds(0, RV)] = hi
        hcat[rows, pl.ds(RV, RV)] = lo
        fcat[rows, :] = flag_v[rows, :].astype(F32).astype(BF)
        return carry

    whole = NODES // CH
    lax.fori_loop(0, whole, split_h, 0)
    rest = pl.ds(whole * CH, NODES - whole * CH)
    hi, lo = split2(hist_v[rest, :])
    hcat[rest, pl.ds(0, RV)] = hi
    hcat[rest, pl.ds(RV, RV)] = lo
    fcat[rest, :] = flag_v[rest, :].astype(F32).astype(BF)
    h_s[...] = dot_t(permt[...], hcat[...])
    w_s[...] = dot_t(permt[:, 0:RV], fcat[...])

    k32[...] = jnp.zeros_like(k32)
    loads[2].wait()
    for a in range(NB):
        row = [stiff_v[a, b] * pat_ref[a, b].astype(F32) for b in range(NB)]
        k32[pl.ds(a * BLK, BLK), pl.ds(0, NODES)] = jnp.concatenate(row, axis=1)

    def split_k(i, carry):
        hi, lo = split2(k32[pl.ds(pl.multiple_of(i * CH, CH), CH), :])
        kk[pl.ds(pl.multiple_of(i * CH, CH), CH), :] = hi
        kk[pl.ds(pl.multiple_of(NP + i * CH, CH), CH), :] = lo
        kk[pl.ds(pl.multiple_of(2 * NP + i * CH, CH), CH), :] = hi
        return carry

    lax.fori_loop(0, NP // CH, split_k, 0)

    def chunks(body):
        def step(i, carry):
            body(i)
            return carry

        lax.fori_loop(0, BW // RC, step, 0, unroll=UNROLL)

    def at(base, i):
        return pl.ds(pl.multiple_of(base + i * RC, RC), RC)

    def partial(k, i, acc):
        part = acc[:, 0:128]
        for n in range(1, NP // 128):
            part = part + acc[:, n * 128 : (n + 1) * 128]
        sums[k, at(0, i), :] = part

    def total(k):
        return jnp.broadcast_to(jnp.sum(sums[k], axis=1, keepdims=True), (BW, 128))

    def wide(k, i):
        return jnp.concatenate([coef[k, at(0, i), :]] * (NP // 128), axis=1)

    def block(b, carry):
        base = b * BW

        def source(i):
            here = at(base, i)
            h = h_s[here, :]
            h2 = h * h
            w = w_s[here, :] * h2 / (1.0 + h2)
            w_s[here, :] = w
            wh = w * h
            acc = jnp.zeros((RC, NP), F32)
            for c in range(COMP):
                rows = at(c * BW, i)
                v = drive[here, pl.ds(c * NP, NP)] - wh * prow[c, 0:RC, :]
                r0_s[rows, :] = v
                acc = acc + v * v
            partial(0, i, acc)

        chunks(source)

        def product(ref, parts):
            v = ref[...]
            hi = v.astype(BF)
            cat = [hi, hi]
            if parts == 3:
                cat.append((v - hi.astype(F32)).astype(BF))
            return dot(jnp.concatenate(cat, axis=1), kk[0 : parts * NP, :])

        im0_s[...] = product(r0_s, 3)

        def first(i):
            tan = 1.5 - w_s[at(base, i), :]
            acc = jnp.zeros((RC, NP), F32)
            for c in range(COMP):
                rows = at(c * BW, i)
                r = r0_s[rows, :]
                im = im0_s[rows, :] + tan * r
                im0_s[rows, :] = im
                acc = acc + r * im
            partial(1, i, acc)

        chunks(first)
        norm0 = total(0)
        size0 = norm0 / jnp.maximum(total(1), 1.0)
        coef[0] = size0

        def first_step(i):
            size = wide(0, i)
            acc = jnp.zeros((RC, NP), F32)
            for c in range(COMP):
                rows = at(c * BW, i)
                r = r0_s[rows, :] - size * im0_s[rows, :]
                r1_s[rows, :] = r
                acc = acc + r * r
            partial(2, i, acc)

        chunks(first_step)
        y_s[...] = product(r1_s, 3)
        norm1 = total(2)
        ratio0 = norm1 / jnp.maximum(norm0, 1.0)
        coef[1] = ratio0

        def second(i):
            tan = 1.5 - w_s[at(base, i), :]
            ratio = wide(1, i)
            acc = jnp.zeros((RC, NP), F32)
            for c in range(COMP):
                rows = at(c * BW, i)
                r = r1_s[rows, :]
                im = y_s[rows, :] + tan * r + ratio * im0_s[rows, :]
                y_s[rows, :] = im
                acc = acc + (r + ratio * r0_s[rows, :]) * im
            partial(3, i, acc)

        chunks(second)
        energy = total(3)
        size1 = norm1 / jnp.maximum(energy, 1.0)
        coef[2] = size1

        def second_step(i):
            size = wide(2, i)
            sq = jnp.zeros((RC, NP), F32)
            cross = jnp.zeros((RC, NP), F32)
            for c in range(COMP):
                rows = at(c * BW, i)
                im = y_s[rows, :]
                r = r1_s[rows, :] - size * im
                r2_s[rows, :] = r
                sq = sq + r * r
                cross = cross + r * im
            partial(4, i, sq)
            partial(5, i, cross)
            partial(6, i, (1.5 - w_s[at(base, i), :]) * sq)

        chunks(second_step)
        y_s[...] = product(r2_s, 2)
        norm2 = total(4)
        ratio1 = norm2 / jnp.maximum(norm1, 1.0)
        rest = total(6) + ratio1 * (2.0 * total(5) + ratio1 * energy)

        def third(i):
            acc = jnp.zeros((RC, NP), F32)
            for c in range(COMP):
                rows = at(c * BW, i)
                r = r2_s[rows, :]
                acc = acc + (2.0 * r - r.astype(BF).astype(F32)) * y_s[rows, :]
            partial(7, i, acc)

        chunks(third)
        a2 = norm2 / jnp.maximum(total(7) + rest, 1.0)
        a1 = size1 + a2 * ratio1
        coef[3] = size0 + a1 * ratio0
        coef[4] = a1
        coef[5] = a2

        def last(i):
            here = at(base, i)
            w = w_s[here, :]
            tan = 1.5 - w
            a = [wide(3 + k, i) for k in range(3)]
            flow = jnp.zeros((RC, NP), F32)
            for c in range(COMP):
                rows = at(c * BW, i)
                x = a[0] * r0_s[rows, :] + a[1] * r1_s[rows, :] + a[2] * r2_s[rows, :]
                flow = flow + prow[c, 0:RC, :] * x
                ycat[here, pl.ds(c * NP, NP)] = tan * x
            h_s[here, :] = h_s[here, :] + w * flow

        chunks(last)

        hi, lo = split2(h_s[pl.ds(pl.multiple_of(base, BW), BW), :])
        ucat[pl.ds(pl.multiple_of(2 * base, BW), BW), :] = hi
        ucat[pl.ds(pl.multiple_of(2 * base + BW, BW), BW), :] = lo

        for k in range(NBLK):
            j = NBLK - 1 - k

            @pl.when(b == k)
            def _():
                t8 = float(CAP) * iota((DEV, BW), 0) + 2.0 * j
                parts = []
                for n in range(k + 1):
                    srow = slotrow[0:1, n * BW : (n + 1) * BW]
                    one = jnp.concatenate(
                        [jnp.where(srow == t8, 1.0, 0.0), jnp.where(srow == t8 + 1.0, 1.0, 0.0)],
                        axis=0,
                    ).astype(BF)
                    parts += [one, one]
                moved = dot(jnp.concatenate(parts, axis=1), ucat[0 : 2 * (k + 1) * BW, :])
                ship[:, 2 * j, :] = moved[0:DEV]
                ship[:, 2 * j + 1, :] = moved[DEV:]
                if k == 0:
                    pl.semaphore_wait(barrier, DEV - 1)

                def send(i, c):
                    peer = lax.rem(me + i * STRIDE, DEV)
                    pltpu.make_async_remote_copy(
                        src_ref=ship.at[peer, pl.ds(2 * j, 2)],
                        dst_ref=recv.at[me, pl.ds(2 * j, 2)],
                        send_sem=send_sem.at[k],
                        recv_sem=recv_sem.at[k],
                        device_id=peer,
                        device_id_type=LOG,
                    ).start()
                    return c

                lax.fori_loop(1, DEV, send, 0, unroll=127)

        return carry

    lax.fori_loop(0, NBLK, block, 0)
    own = pltpu.make_async_copy(ship.at[me], recv.at[me], loc_sem)
    own.start()

    strain_p = dot_t(s32[...], servest[...])
    delta = jnp.zeros((8, RV), F32)
    for c in range(COMP):
        lanes = pl.ds(c * NP, NP)
        hi, lo = split2(ycat[:, lanes])
        with_hi = dot_t(gmat[:, lanes], hi)
        delta += with_hi[0:8] + with_hi[8:16] + dot_t(gmat[:, lanes], lo)[0:8]
    stress = strain_p[8:16] + strain_p[16:24] + strain_p[24:32]
    stress = stress + delta * (1.0 / math.sqrt(COMP * NODES))
    back = dot(stack(split3(stress)), servest[...])
    stress_ref[...] = (back[0:8] + back[8:16] + back[16:24])[0:VOIGT]
    own.wait()
    for k in range(NBLK):
        two_rows = pl.ds(2 * (NBLK - 1 - k), 2)
        some = pl.ds(0, DEV - 1)
        pltpu.make_async_copy(ship.at[some, two_rows], recv.at[some, two_rows], recv_sem.at[k]).wait()
        pltpu.make_async_copy(ship.at[some, two_rows], recv.at[some, two_rows], send_sem.at[k]).wait()


def turn(raw_ref, raw_stress_ref, out_hbm, stress_ref, buf, sem):
    stress_ref[...] = raw_stress_ref[...]
    copies = []
    for i in range(DEV * CAP // OUTW):
        for k in range(OUTW // BW):
            first = i * OUTW + k * BW
            piece = raw_ref[pl.ds(first // CAP, BW // CAP)].reshape(BW, NP)
            buf[:, pl.ds(first, BW)] = jnp.transpose(piece)[0:NODES]
        part = pl.ds(i * OUTW, OUTW)
        copies.append(pltpu.make_async_copy(buf.at[:, part], out_hbm.at[:, part], sem.at[i]))
        copies[i].start()
    for copy in copies:
        copy.wait()


def shards(
    history, yield_flags, strain, qp_to_rve, new_owner, stiffness, pattern, coupling, plastic_dir
):
    owner = new_owner.reshape(1, RV)
    hbm = pl.BlockSpec(memory_space=pl.ANY)
    vmem = pl.BlockSpec(memory_space=pltpu.VMEM)
    v = pltpu.VMEM
    raw, raw_stress = pl.pallas_call(
        kernel,
        out_shape=(
            v((DEV, CAP, NP), F32),
            v((VOIGT, RV), F32),
        ),
        in_specs=[hbm] * 6 + [pl.BlockSpec(memory_space=pltpu.SMEM)] + [hbm] * 2,
        out_specs=(vmem, vmem),
        scratch_shapes=[
            v((NODES, RV), F32), v((NODES, RV), jnp.int32), v((VOIGT, RV), F32),
            v((1, RV), jnp.int32), v((1, RV), jnp.int32), v((NB, NB, BLK, BLK), F32),
            v((COMP, VOIGT, NODES), F32), v((COMP, NODES), F32),
            v((NP, NP), F32), v((3 * NP, NP), BF), v((NP, 2 * RV), BF), v((NP, RV), BF),
            v((8, RV), F32), v((32, RV), BF), v((RV, 2 * RV), BF), v((RV, RV), BF),
            v((RV, COMP * NP), F32), v((COMP, 8, NP), F32), v((16, COMP * NP), BF),
            v((RV, NP), F32), v((RV, NP), F32),
            v((COMP * BW, NP), F32), v((COMP * BW, NP), F32), v((COMP * BW, NP), F32),
            v((COMP * BW, NP), F32), v((COMP * BW, NP), F32),
            v((RV, COMP * NP), F32), v((2 * RV, NP), BF), v((6, BW, 128), F32), v((8, BW, 128), F32),
            v((DEV, CAP, NP), F32),
            pltpu.SemaphoreType.DMA((8,)), pltpu.SemaphoreType.DMA(()),
            pltpu.SemaphoreType.DMA((NBLK,)), pltpu.SemaphoreType.DMA((NBLK,)),
        ],
        compiler_params=pltpu.CompilerParams(
            collective_id=0, has_side_effects=True, vmem_limit_bytes=56 * 1024 * 1024
        ),
        name="micro_newton",
    )(
        history, yield_flags, strain, qp_to_rve, owner, stiffness, pattern, coupling, plastic_dir
    )
    return pl.pallas_call(
        turn,
        out_shape=(
            jax.ShapeDtypeStruct((NODES, DEV * CAP), F32),
            jax.ShapeDtypeStruct((VOIGT, RV), F32),
        ),
        in_specs=[vmem, vmem],
        out_specs=(hbm, vmem),
        scratch_shapes=[
            v((NODES, DEV * CAP), F32), pltpu.SemaphoreType.DMA((DEV * CAP // OUTW,)),
        ],
        compiler_params=pltpu.CompilerParams(vmem_limit_bytes=16 * 1024 * 1024),
        name="turn_history",
    )(raw, raw_stress)


def solution(mesh):
    both = ("macro", "pool")
    return jax.shard_map(
        shards,
        mesh=mesh,
        in_specs=(
            P(None, both), P(None, both), P(None, both), P(both, None), P(both, None),
            P(), P(), P(), P(),
        ),
        out_specs=(P(None, both), P(None, both)),
        check_vma=False,
    )
```

```python
import functools
import math

import jax
import jax.numpy as jnp
from jax import lax
from jax.experimental import pallas as pl
from jax.experimental.pallas import tpu as pltpu
from jax.sharding import PartitionSpec as P

ITERS = 3
NB = 9
BLK = 81
COMP = 3
VOIGT = 6
NODES = NB * BLK
NP = 768
RV = 512
BW = 128
NBLK = RV // BW
MACRO = 16
POOL = 8
DEV = MACRO * POOL
CAP = 8
CH = 64
RC = 8
UNROLL = 16
OUTW = 256
STRIDE = 77
LOG = pl.DeviceIdType.LOGICAL
F32 = jnp.float32
BF = jnp.bfloat16


def split2(x):
    hi = x.astype(BF)
    return hi, (x - hi.astype(F32)).astype(BF)


def split3(x):
    hi = x.astype(BF)
    rest = x - hi.astype(F32)
    mid = rest.astype(BF)
    return hi, mid, (rest - mid.astype(F32)).astype(BF)


def dot(a, b):
    return jnp.dot(a, b, preferred_element_type=F32)


def to_columns(row):
    return jnp.transpose(jnp.broadcast_to(row, (BW, RV)))


def iota(shape, dim):
    return lax.broadcasted_iota(jnp.int32, shape, dim).astype(F32)


def dot_t(a, b):
    return lax.dot_general(a, b, (((1,), (1,)), ((), ())), preferred_element_type=F32)


def stack(parts):
    return jnp.concatenate([p.astype(F32) for p in parts], axis=0).astype(BF)


def kernel(
    hist_hbm, flag_hbm, strain_hbm, qp_hbm, owner_hbm, stiff_hbm, pat_ref, coup_hbm, plast_hbm,
    recv, stress_ref,
    hist_v, flag_v, strain_v, qp_v, owner_v, stiff_v, coup_v, plast_v,
    k32, kk, hcat, fcat, slotrow, s32, permt, servest, drive, prow, gmat,
    h_s, w_s, r0_s, r1_s, r2_s, im0_s, y_s, ycat, ucat, coef, sums, ship,
    in_sem, loc_sem, send_sem, recv_sem, column_sem,
):
    me = lax.axis_index("macro") * POOL + lax.axis_index("pool")
    loads = {}

    def load(name, src, dst, sem):
        loads.setdefault(name, []).append(pltpu.make_async_copy(src, dst, in_sem.at[sem]))
        loads[name][-1].start()

    def loaded(*names):
        for name in names:
            for copy in loads[name]:
                copy.wait()

    load("owner", owner_hbm, owner_v, 0)
    load("qp", qp_hbm, qp_v, 1)
    load("small", strain_hbm, strain_v, 2)
    load("small", coup_hbm, coup_v, 3)
    load("small", plast_hbm, plast_v, 4)
    for i, (start, size) in enumerate(((0, 256), (256, 256), (512, NODES - 512))):
        rows = pl.ds(start, size)
        load("hist", hist_hbm.at[rows], hist_v.at[rows], 5 + i)
        load("flag", flag_hbm.at[rows], flag_v.at[rows], 8 + i)
    for a in range(NB):
        load("stiff%d" % a, stiff_hbm.at[a], stiff_v.at[a], 11 + a)

    barrier = pltpu.get_barrier_semaphore()

    macro, pool = lax.axis_index("macro"), lax.axis_index("pool")

    def greet(sem, other_macro, other_pool):
        pl.semaphore_signal(
            sem, inc=1, device_id=other_macro * POOL + other_pool, device_id_type=LOG
        )

    for i in range(1, POOL):
        greet(barrier, macro, lax.rem(pool + i, POOL))
    for i in range(1, MACRO):
        greet(barrier, lax.rem(macro + i, MACRO), pool)

    loaded("owner", "qp")
    owner_row = owner_v[...].astype(F32)
    owner_col = to_columns(owner_row)
    qp_row = qp_v[...].astype(F32)
    e_col = iota((RV, BW), 0)
    rank_part = jnp.zeros((RV, BW), F32)
    rank_rows = []
    for t in range(NBLK):
        e_row = iota((RV, BW), 1) + float(t * BW)
        same = owner_col == owner_row[:, t * BW : (t + 1) * BW]
        rank_part += jnp.where(same & (e_row < e_col), 1.0, 0.0)
        rank_rows.append(
            jnp.sum(jnp.where(same & (e_col < e_row), 1.0, 0.0), axis=0, keepdims=True)
        )
    rank_col = jnp.broadcast_to(jnp.sum(rank_part, axis=1, keepdims=True), (RV, BW))
    key_col = rank_col * float(RV) - e_col
    e_part = jnp.zeros((RV, BW), F32)
    slot_part = jnp.zeros((RV, BW), F32)
    for t in range(NBLK):
        lanes = pl.ds(t * BW, BW)
        e_row = iota((1, BW), 1) + float(t * BW)
        key_row = rank_rows[t] * float(RV) - e_row
        pos_row = jnp.sum(jnp.where(key_col > key_row, 1.0, 0.0), axis=0, keepdims=True)
        slot_row = owner_row[:, t * BW : (t + 1) * BW] * float(CAP) + rank_rows[t]
        chosen = iota((RV, BW), 0) == pos_row
        e_part += jnp.where(chosen, e_row, 0.0)
        slot_part += jnp.where(chosen, slot_row, 0.0)
        one = jnp.where(chosen, 1.0, 0.0).astype(BF)
        permt[:, lanes] = one
        permt[:, pl.ds(RV + t * BW, BW)] = one
    e_of = jnp.broadcast_to(jnp.sum(e_part, axis=1, keepdims=True), (RV, BW))
    slot_of = jnp.broadcast_to(jnp.sum(slot_part, axis=1, keepdims=True), (RV, BW))
    slotrow[...] = jnp.transpose(slot_of)[0:8]
    for t in range(NBLK):
        lanes = pl.ds(t * BW, BW)
        hit = e_of == qp_row[:, t * BW : (t + 1) * BW]
        servest[:, lanes] = jnp.where(hit, 1.0, 0.0).astype(BF)

    loaded("small")
    shi, smid, slo = split3(jnp.concatenate([strain_v[...], jnp.zeros((2, RV), F32)], axis=0))
    s32[...] = stack([shi, shi, smid, slo])
    strain_t = dot_t(servest[...], s32[...]).astype(BF)
    edge = jnp.zeros((2, NODES), F32)
    pad = jnp.zeros((CAP, NP - NODES), F32)
    cols = []
    for c in range(COMP):
        coup = jnp.concatenate([jnp.concatenate([coup_v[c], edge], axis=0), pad], axis=1)
        chi = coup.astype(BF).astype(F32)
        clo = coup - chi
        gmat[:, pl.ds(c * NP, NP)] = jnp.concatenate([chi, clo], axis=0).astype(BF)
        cols.append(jnp.concatenate([chi, clo, chi, jnp.zeros((8, NP), F32)], axis=0))
        line = jnp.concatenate([plast_v[pl.ds(c, 1), :], pad[0:1]], axis=1)
        prow[c] = jnp.broadcast_to(line, (8, NP))
    drive[...] = dot(strain_t, jnp.concatenate(cols, axis=1).astype(BF))

    loaded("hist", "flag")
    hcat[pl.ds(NP - 64, 64), :] = jnp.zeros((64, 2 * RV), BF)
    fcat[pl.ds(NP - 64, 64), :] = jnp.zeros((64, RV), BF)

    def split_h(i, carry):
        rows = pl.ds(pl.multiple_of(i * CH, CH), CH)
        hi, lo = split2(hist_v[rows, :])
        hcat[rows, pl.ds(0, RV)] = hi
        hcat[rows, pl.ds(RV, RV)] = lo
        fcat[rows, :] = flag_v[rows, :].astype(F32).astype(BF)
        return carry

    whole = NODES // CH
    lax.fori_loop(0, whole, split_h, 0)
    rest = pl.ds(whole * CH, NODES - whole * CH)
    hi, lo = split2(hist_v[rest, :])
    hcat[rest, pl.ds(0, RV)] = hi
    hcat[rest, pl.ds(RV, RV)] = lo
    fcat[rest, :] = flag_v[rest, :].astype(F32).astype(BF)
    h_s[...] = dot_t(permt[...], hcat[...])
    w_s[...] = dot_t(permt[:, 0:RV], fcat[...])

    pl.semaphore_wait(barrier, POOL + MACRO - 2)
    for i in range(1, MACRO):
        greet(column_sem, lax.rem(macro + i, MACRO), pool)

    k32[...] = jnp.zeros_like(k32)
    for a in range(NB):
        loaded("stiff%d" % a)
        row = [stiff_v[a, b] * pat_ref[a, b].astype(F32) for b in range(NB)]
        k32[pl.ds(a * BLK, BLK), pl.ds(0, NODES)] = jnp.concatenate(row, axis=1)

    def split_k(i, carry):
        hi, lo = split2(k32[pl.ds(pl.multiple_of(i * CH, CH), CH), :])
        kk[pl.ds(pl.multiple_of(i * CH, CH), CH), :] = hi
        kk[pl.ds(pl.multiple_of(NP + i * CH, CH), CH), :] = lo
        kk[pl.ds(pl.multiple_of(2 * NP + i * CH, CH), CH), :] = hi
        return carry

    lax.fori_loop(0, NP // CH, split_k, 0)

    def chunks(body):
        def step(i, carry):
            body(i)
            return carry

        lax.fori_loop(0, BW // RC, step, 0, unroll=UNROLL)

    def at(base, i):
        return pl.ds(pl.multiple_of(base + i * RC, RC), RC)

    def partial(k, i, acc):
        part = acc[:, 0:128]
        for n in range(1, NP // 128):
            part = part + acc[:, n * 128 : (n + 1) * 128]
        sums[k, at(0, i), :] = part

    def total(k):
        return jnp.broadcast_to(jnp.sum(sums[k], axis=1, keepdims=True), (BW, 128))

    def wide(k, i):
        return jnp.concatenate([coef[k, at(0, i), :]] * (NP // 128), axis=1)

    def block(b, carry):
        base = b * BW

        def source(i):
            here = at(base, i)
            h = h_s[here, :]
            h2 = h * h
            w = w_s[here, :] * h2 / (1.0 + h2)
            w_s[here, :] = w
            wh = w * h
            acc = jnp.zeros((RC, NP), F32)
            for c in range(COMP):
                rows = at(c * BW, i)
                v = drive[here, pl.ds(c * NP, NP)] - wh * prow[c, 0:RC, :]
                r0_s[rows, :] = v
                acc = acc + v * v
            partial(0, i, acc)

        chunks(source)

        def product(ref, parts):
            v = ref[...]
            hi = v.astype(BF)
            cat = [hi, hi]
            if parts == 3:
                cat.append((v - hi.astype(F32)).astype(BF))
            return dot(jnp.concatenate(cat, axis=1), kk[0 : parts * NP, :])

        im0_s[...] = product(r0_s, 3)

        def first(i):
            tan = 1.5 - w_s[at(base, i), :]
            acc = jnp.zeros((RC, NP), F32)
            for c in range(COMP):
                rows = at(c * BW, i)
                r = r0_s[rows, :]
                im = im0_s[rows, :] + tan * r
                im0_s[rows, :] = im
                acc = acc + r * im
            partial(1, i, acc)

        chunks(first)
        norm0 = total(0)
        size0 = norm0 / jnp.maximum(total(1), 1.0)
        coef[0] = size0

        def first_step(i):
            size = wide(0, i)
            acc = jnp.zeros((RC, NP), F32)
            for c in range(COMP):
                rows = at(c * BW, i)
                r = r0_s[rows, :] - size * im0_s[rows, :]
                r1_s[rows, :] = r
                acc = acc + r * r
            partial(2, i, acc)

        chunks(first_step)
        y_s[...] = product(r1_s, 3)
        norm1 = total(2)
        ratio0 = norm1 / jnp.maximum(norm0, 1.0)
        coef[1] = ratio0

        def second(i):
            tan = 1.5 - w_s[at(base, i), :]
            ratio = wide(1, i)
            acc = jnp.zeros((RC, NP), F32)
            for c in range(COMP):
                rows = at(c * BW, i)
                r = r1_s[rows, :]
                im = y_s[rows, :] + tan * r + ratio * im0_s[rows, :]
                y_s[rows, :] = im
                acc = acc + (r + ratio * r0_s[rows, :]) * im
            partial(3, i, acc)

        chunks(second)
        energy = total(3)
        size1 = norm1 / jnp.maximum(energy, 1.0)
        coef[2] = size1

        def second_step(i):
            size = wide(2, i)
            sq = jnp.zeros((RC, NP), F32)
            cross = jnp.zeros((RC, NP), F32)
            for c in range(COMP):
                rows = at(c * BW, i)
                im = y_s[rows, :]
                r = r1_s[rows, :] - size * im
                r2_s[rows, :] = r
                sq = sq + r * r
                cross = cross + r * im
            partial(4, i, sq)
            partial(5, i, cross)
            partial(6, i, (1.5 - w_s[at(base, i), :]) * sq)

        chunks(second_step)
        y_s[...] = product(r2_s, 2)
        norm2 = total(4)
        ratio1 = norm2 / jnp.maximum(norm1, 1.0)
        rest = total(6) + ratio1 * (2.0 * total(5) + ratio1 * energy)

        def third(i):
            acc = jnp.zeros((RC, NP), F32)
            for c in range(COMP):
                rows = at(c * BW, i)
                r = r2_s[rows, :]
                acc = acc + (2.0 * r - r.astype(BF).astype(F32)) * y_s[rows, :]
            partial(7, i, acc)

        chunks(third)
        a2 = norm2 / jnp.maximum(total(7) + rest, 1.0)
        a1 = size1 + a2 * ratio1
        coef[3] = size0 + a1 * ratio0
        coef[4] = a1
        coef[5] = a2

        def last(i):
            here = at(base, i)
            w = w_s[here, :]
            tan = 1.5 - w
            a = [wide(3 + k, i) for k in range(3)]
            flow = jnp.zeros((RC, NP), F32)
            for c in range(COMP):
                rows = at(c * BW, i)
                x = a[0] * r0_s[rows, :] + a[1] * r1_s[rows, :] + a[2] * r2_s[rows, :]
                flow = flow + prow[c, 0:RC, :] * x
                ycat[here, pl.ds(c * NP, NP)] = tan * x
            h_s[here, :] = h_s[here, :] + w * flow

        chunks(last)

        hi, lo = split2(h_s[pl.ds(pl.multiple_of(base, BW), BW), :])
        ucat[pl.ds(pl.multiple_of(2 * base, BW), BW), :] = hi
        ucat[pl.ds(pl.multiple_of(2 * base + BW, BW), BW), :] = lo

        for k in range(NBLK):
            j = NBLK - 1 - k

            @pl.when(b == k)
            def _():
                t8 = float(CAP) * iota((DEV, BW), 0) + 2.0 * j
                parts = []
                for n in range(k + 1):
                    srow = slotrow[0:1, n * BW : (n + 1) * BW]
                    one = jnp.concatenate(
                        [jnp.where(srow == t8, 1.0, 0.0), jnp.where(srow == t8 + 1.0, 1.0, 0.0)],
                        axis=0,
                    ).astype(BF)
                    parts += [one, one]
                moved = dot(jnp.concatenate(parts, axis=1), ucat[0 : 2 * (k + 1) * BW, :])
                ship[:, 2 * j, :] = moved[0:DEV]
                ship[:, 2 * j + 1, :] = moved[DEV:]
                if k == 0:
                    pl.semaphore_wait(column_sem, MACRO - 1)

                def send(i, c):
                    peer = lax.rem(me + i * STRIDE, DEV)
                    pltpu.make_async_remote_copy(
                        src_ref=ship.at[peer, pl.ds(2 * j, 2)],
                        dst_ref=recv.at[me, pl.ds(2 * j, 2)],
                        send_sem=send_sem.at[k],
                        recv_sem=recv_sem.at[k],
                        device_id=peer,
                        device_id_type=LOG,
                    ).start()
                    return c

                lax.fori_loop(1, DEV, send, 0, unroll=127)

        return carry

    lax.fori_loop(0, NBLK, block, 0)
    own = pltpu.make_async_copy(ship.at[me], recv.at[me], loc_sem)
    own.start()

    strain_p = dot_t(s32[...], servest[...])
    delta = jnp.zeros((8, RV), F32)
    for c in range(COMP):
        lanes = pl.ds(c * NP, NP)
        hi, lo = split2(ycat[:, lanes])
        with_hi = dot_t(gmat[:, lanes], hi)
        delta += with_hi[0:8] + with_hi[8:16] + dot_t(gmat[:, lanes], lo)[0:8]
    stress = strain_p[8:16] + strain_p[16:24] + strain_p[24:32]
    stress = stress + delta * (1.0 / math.sqrt(COMP * NODES))
    back = dot(stack(split3(stress)), servest[...])
    stress_ref[...] = (back[0:8] + back[8:16] + back[16:24])[0:VOIGT]
    own.wait()
    for k in range(NBLK):
        two_rows = pl.ds(2 * (NBLK - 1 - k), 2)
        some = pl.ds(0, DEV - 1)
        pltpu.make_async_copy(ship.at[some, two_rows], recv.at[some, two_rows], recv_sem.at[k]).wait()
        pltpu.make_async_copy(ship.at[some, two_rows], recv.at[some, two_rows], send_sem.at[k]).wait()


def turn(raw_ref, raw_stress_ref, out_hbm, stress_ref, buf, sem):
    stress_ref[...] = raw_stress_ref[...]
    copies = []
    for i in range(DEV * CAP // OUTW):
        for k in range(OUTW // BW):
            first = i * OUTW + k * BW
            piece = raw_ref[pl.ds(first // CAP, BW // CAP)].reshape(BW, NP)
            buf[:, pl.ds(first, BW)] = jnp.transpose(piece)[0:NODES]
        part = pl.ds(i * OUTW, OUTW)
        copies.append(pltpu.make_async_copy(buf.at[:, part], out_hbm.at[:, part], sem.at[i]))
        copies[i].start()
    for copy in copies:
        copy.wait()


def shards(
    history, yield_flags, strain, qp_to_rve, new_owner, stiffness, pattern, coupling, plastic_dir
):
    owner = new_owner.reshape(1, RV)
    hbm = pl.BlockSpec(memory_space=pl.ANY)
    vmem = pl.BlockSpec(memory_space=pltpu.VMEM)
    v = pltpu.VMEM
    raw, raw_stress = pl.pallas_call(
        kernel,
        out_shape=(
            v((DEV, CAP, NP), F32),
            v((VOIGT, RV), F32),
        ),
        in_specs=[hbm] * 6 + [pl.BlockSpec(memory_space=pltpu.SMEM)] + [hbm] * 2,
        out_specs=(vmem, vmem),
        scratch_shapes=[
            v((NODES, RV), F32), v((NODES, RV), jnp.int32), v((VOIGT, RV), F32),
            v((1, RV), jnp.int32), v((1, RV), jnp.int32), v((NB, NB, BLK, BLK), F32),
            v((COMP, VOIGT, NODES), F32), v((COMP, NODES), F32),
            v((NP, NP), F32), v((3 * NP, NP), BF), v((NP, 2 * RV), BF), v((NP, RV), BF),
            v((8, RV), F32), v((32, RV), BF), v((RV, 2 * RV), BF), v((RV, RV), BF),
            v((RV, COMP * NP), F32), v((COMP, 8, NP), F32), v((16, COMP * NP), BF),
            v((RV, NP), F32), v((RV, NP), F32),
            v((COMP * BW, NP), F32), v((COMP * BW, NP), F32), v((COMP * BW, NP), F32),
            v((COMP * BW, NP), F32), v((COMP * BW, NP), F32),
            v((RV, COMP * NP), F32), v((2 * RV, NP), BF), v((6, BW, 128), F32), v((8, BW, 128), F32),
            v((DEV, CAP, NP), F32),
            pltpu.SemaphoreType.DMA((20,)), pltpu.SemaphoreType.DMA(()),
            pltpu.SemaphoreType.DMA((NBLK,)), pltpu.SemaphoreType.DMA((NBLK,)),
            pltpu.SemaphoreType.REGULAR,
        ],
        compiler_params=pltpu.CompilerParams(
            collective_id=0, has_side_effects=True, vmem_limit_bytes=56 * 1024 * 1024
        ),
        name="micro_newton",
    )(
        history, yield_flags, strain, qp_to_rve, owner, stiffness, pattern, coupling, plastic_dir
    )
    return pl.pallas_call(
        turn,
        out_shape=(
            jax.ShapeDtypeStruct((NODES, DEV * CAP), F32),
            jax.ShapeDtypeStruct((VOIGT, RV), F32),
        ),
        in_specs=[vmem, vmem],
        out_specs=(hbm, vmem),
        scratch_shapes=[
            v((NODES, DEV * CAP), F32), pltpu.SemaphoreType.DMA((DEV * CAP // OUTW,)),
        ],
        compiler_params=pltpu.CompilerParams(vmem_limit_bytes=16 * 1024 * 1024),
        name="turn_history",
    )(raw, raw_stress)


def solution(mesh):
    both = ("macro", "pool")
    return jax.shard_map(
        shards,
        mesh=mesh,
        in_specs=(
            P(None, both), P(None, both), P(None, both), P(both, None), P(both, None),
            P(), P(), P(), P(),
        ),
        out_specs=(P(None, both), P(None, both)),
        check_vma=False,
    )
```

```python
import functools
import math

import jax
import jax.numpy as jnp
from jax import lax
from jax.experimental import pallas as pl
from jax.experimental.pallas import tpu as pltpu
from jax.sharding import PartitionSpec as P

ITERS = 3
NB = 9
BLK = 81
COMP = 3
VOIGT = 6
NODES = NB * BLK
NP = 768
RV = 512
BW = 128
NBLK = RV // BW
MACRO = 16
POOL = 8
DEV = MACRO * POOL
CAP = 8
CH = 64
RC = 8
UNROLL = 16
OUTW = 256
STRIDE = 109
LOG = pl.DeviceIdType.LOGICAL
F32 = jnp.float32
BF = jnp.bfloat16


def split2(x):
    hi = x.astype(BF)
    return hi, (x - hi.astype(F32)).astype(BF)


def split3(x):
    hi = x.astype(BF)
    rest = x - hi.astype(F32)
    mid = rest.astype(BF)
    return hi, mid, (rest - mid.astype(F32)).astype(BF)


def dot(a, b):
    return jnp.dot(a, b, preferred_element_type=F32)


def to_columns(row):
    return jnp.transpose(jnp.broadcast_to(row, (BW, RV)))


def iota(shape, dim):
    return lax.broadcasted_iota(jnp.int32, shape, dim).astype(F32)


def dot_t(a, b):
    return lax.dot_general(a, b, (((1,), (1,)), ((), ())), preferred_element_type=F32)


def stack(parts):
    return jnp.concatenate([p.astype(F32) for p in parts], axis=0).astype(BF)


def kernel(
    hist_hbm, flag_hbm, strain_hbm, qp_hbm, owner_hbm, stiff_hbm, pat_ref, coup_hbm, plast_hbm,
    recv, stress_ref,
    hist_v, flag_v, strain_v, qp_v, owner_v, stiff_v, coup_v, plast_v,
    k32, kk, hcat, fcat, slotrow, s32, permt, servest, drive, prow, gmat,
    h_s, w_s, r0_s, r1_s, r2_s, im0_s, y_s, ycat, ucat, coef, sums, ship,
    in_sem, loc_sem, send_sem, recv_sem, column_sem,
):
    me = lax.axis_index("macro") * POOL + lax.axis_index("pool")
    loads = {}

    def load(name, src, dst, sem):
        loads.setdefault(name, []).append(pltpu.make_async_copy(src, dst, in_sem.at[sem]))
        loads[name][-1].start()

    def loaded(*names):
        for name in names:
            for copy in loads[name]:
                copy.wait()

    load("owner", owner_hbm, owner_v, 0)
    load("qp", qp_hbm, qp_v, 1)
    load("small", strain_hbm, strain_v, 2)
    load("small", coup_hbm, coup_v, 3)
    load("small", plast_hbm, plast_v, 4)
    for i, (start, size) in enumerate(((0, 256), (256, 256), (512, NODES - 512))):
        rows = pl.ds(start, size)
        load("hist", hist_hbm.at[rows], hist_v.at[rows], 5 + i)
        load("flag", flag_hbm.at[rows], flag_v.at[rows], 8 + i)
    for a in range(NB):
        load("stiff%d" % a, stiff_hbm.at[a], stiff_v.at[a], 11 + a)

    barrier = pltpu.get_barrier_semaphore()

    macro, pool = lax.axis_index("macro"), lax.axis_index("pool")

    def greet(sem, other_macro, other_pool):
        pl.semaphore_signal(
            sem, inc=1, device_id=other_macro * POOL + other_pool, device_id_type=LOG
        )

    for i in range(1, POOL):
        greet(barrier, macro, lax.rem(pool + i, POOL))
    for i in range(1, MACRO):
        greet(barrier, lax.rem(macro + i, MACRO), pool)

    loaded("owner", "qp")
    owner_row = owner_v[...].astype(F32)
    owner_col = to_columns(owner_row)
    qp_row = qp_v[...].astype(F32)
    e_col = iota((RV, BW), 0)
    rank_part = jnp.zeros((RV, BW), F32)
    rank_rows = []
    for t in range(NBLK):
        e_row = iota((RV, BW), 1) + float(t * BW)
        same = owner_col == owner_row[:, t * BW : (t + 1) * BW]
        rank_part += jnp.where(same & (e_row < e_col), 1.0, 0.0)
        rank_rows.append(
            jnp.sum(jnp.where(same & (e_col < e_row), 1.0, 0.0), axis=0, keepdims=True)
        )
    rank_col = jnp.broadcast_to(jnp.sum(rank_part, axis=1, keepdims=True), (RV, BW))
    key_col = rank_col * float(RV) - e_col
    e_part = jnp.zeros((RV, BW), F32)
    slot_part = jnp.zeros((RV, BW), F32)
    for t in range(NBLK):
        lanes = pl.ds(t * BW, BW)
        e_row = iota((1, BW), 1) + float(t * BW)
        key_row = rank_rows[t] * float(RV) - e_row
        pos_row = jnp.sum(jnp.where(key_col > key_row, 1.0, 0.0), axis=0, keepdims=True)
        slot_row = owner_row[:, t * BW : (t + 1) * BW] * float(CAP) + rank_rows[t]
        chosen = iota((RV, BW), 0) == pos_row
        e_part += jnp.where(chosen, e_row, 0.0)
        slot_part += jnp.where(chosen, slot_row, 0.0)
        one = jnp.where(chosen, 1.0, 0.0).astype(BF)
        permt[:, lanes] = one
        permt[:, pl.ds(RV + t * BW, BW)] = one
    e_of = jnp.broadcast_to(jnp.sum(e_part, axis=1, keepdims=True), (RV, BW))
    slot_of = jnp.broadcast_to(jnp.sum(slot_part, axis=1, keepdims=True), (RV, BW))
    slotrow[...] = jnp.transpose(slot_of)[0:8]
    for t in range(NBLK):
        lanes = pl.ds(t * BW, BW)
        hit = e_of == qp_row[:, t * BW : (t + 1) * BW]
        servest[:, lanes] = jnp.where(hit, 1.0, 0.0).astype(BF)

    loaded("small")
    shi, smid, slo = split3(jnp.concatenate([strain_v[...], jnp.zeros((2, RV), F32)], axis=0))
    s32[...] = stack([shi, shi, smid, slo])
    strain_t = dot_t(servest[...], s32[...]).astype(BF)
    edge = jnp.zeros((2, NODES), F32)
    pad = jnp.zeros((CAP, NP - NODES), F32)
    cols = []
    for c in range(COMP):
        coup = jnp.concatenate([jnp.concatenate([coup_v[c], edge], axis=0), pad], axis=1)
        chi = coup.astype(BF).astype(F32)
        clo = coup - chi
        gmat[:, pl.ds(c * NP, NP)] = jnp.concatenate([chi, clo], axis=0).astype(BF)
        cols.append(jnp.concatenate([chi, clo, chi, jnp.zeros((8, NP), F32)], axis=0))
        line = jnp.concatenate([plast_v[pl.ds(c, 1), :], pad[0:1]], axis=1)
        prow[c] = jnp.broadcast_to(line, (8, NP))
    drive[...] = dot(strain_t, jnp.concatenate(cols, axis=1).astype(BF))

    loaded("hist", "flag")
    hcat[pl.ds(NP - 64, 64), :] = jnp.zeros((64, 2 * RV), BF)
    fcat[pl.ds(NP - 64, 64), :] = jnp.zeros((64, RV), BF)

    def split_h(i, carry):
        rows = pl.ds(pl.multiple_of(i * CH, CH), CH)
        hi, lo = split2(hist_v[rows, :])
        hcat[rows, pl.ds(0, RV)] = hi
        hcat[rows, pl.ds(RV, RV)] = lo
        fcat[rows, :] = flag_v[rows, :].astype(F32).astype(BF)
        return carry

    whole = NODES // CH
    lax.fori_loop(0, whole, split_h, 0)
    rest = pl.ds(whole * CH, NODES - whole * CH)
    hi, lo = split2(hist_v[rest, :])
    hcat[rest, pl.ds(0, RV)] = hi
    hcat[rest, pl.ds(RV, RV)] = lo
    fcat[rest, :] = flag_v[rest, :].astype(F32).astype(BF)
    h_s[...] = dot_t(permt[...], hcat[...])
    w_s[...] = dot_t(permt[:, 0:RV], fcat[...])

    pl.semaphore_wait(barrier, POOL + MACRO - 2)
    for i in range(1, MACRO):
        greet(column_sem, lax.rem(macro + i, MACRO), pool)

    k32[...] = jnp.zeros_like(k32)
    for a in range(NB):
        loaded("stiff%d" % a)
        row = [stiff_v[a, b] * pat_ref[a, b].astype(F32) for b in range(NB)]
        k32[pl.ds(a * BLK, BLK), pl.ds(0, NODES)] = jnp.concatenate(row, axis=1)

    def split_k(i, carry):
        hi, lo = split2(k32[pl.ds(pl.multiple_of(i * CH, CH), CH), :])
        kk[pl.ds(pl.multiple_of(i * CH, CH), CH), :] = hi
        kk[pl.ds(pl.multiple_of(NP + i * CH, CH), CH), :] = lo
        kk[pl.ds(pl.multiple_of(2 * NP + i * CH, CH), CH), :] = hi
        return carry

    lax.fori_loop(0, NP // CH, split_k, 0)

    def chunks(body):
        def step(i, carry):
            body(i)
            return carry

        lax.fori_loop(0, BW // RC, step, 0, unroll=UNROLL)

    def at(base, i):
        return pl.ds(pl.multiple_of(base + i * RC, RC), RC)

    def partial(k, i, acc):
        part = acc[:, 0:128]
        for n in range(1, NP // 128):
            part = part + acc[:, n * 128 : (n + 1) * 128]
        sums[k, at(0, i), :] = part

    def total(k):
        return jnp.broadcast_to(jnp.sum(sums[k], axis=1, keepdims=True), (BW, 128))

    def wide(k, i):
        return jnp.concatenate([coef[k, at(0, i), :]] * (NP // 128), axis=1)

    def block(b, carry):
        base = b * BW

        def source(i):
            here = at(base, i)
            h = h_s[here, :]
            h2 = h * h
            w = w_s[here, :] * h2 / (1.0 + h2)
            w_s[here, :] = w
            wh = w * h
            acc = jnp.zeros((RC, NP), F32)
            for c in range(COMP):
                rows = at(c * BW, i)
                v = drive[here, pl.ds(c * NP, NP)] - wh * prow[c, 0:RC, :]
                r0_s[rows, :] = v
                acc = acc + v * v
            partial(0, i, acc)

        chunks(source)

        def product(ref, parts):
            v = ref[...]
            hi = v.astype(BF)
            cat = [hi, hi]
            if parts == 3:
                cat.append((v - hi.astype(F32)).astype(BF))
            return dot(jnp.concatenate(cat, axis=1), kk[0 : parts * NP, :])

        im0_s[...] = product(r0_s, 3)

        def first(i):
            tan = 1.5 - w_s[at(base, i), :]
            acc = jnp.zeros((RC, NP), F32)
            for c in range(COMP):
                rows = at(c * BW, i)
                r = r0_s[rows, :]
                im = im0_s[rows, :] + tan * r
                im0_s[rows, :] = im
                acc = acc + r * im
            partial(1, i, acc)

        chunks(first)
        norm0 = total(0)
        size0 = norm0 / jnp.maximum(total(1), 1.0)
        coef[0] = size0

        def first_step(i):
            size = wide(0, i)
            acc = jnp.zeros((RC, NP), F32)
            for c in range(COMP):
                rows = at(c * BW, i)
                r = r0_s[rows, :] - size * im0_s[rows, :]
                r1_s[rows, :] = r
                acc = acc + r * r
            partial(2, i, acc)

        chunks(first_step)
        y_s[...] = product(r1_s, 3)
        norm1 = total(2)
        ratio0 = norm1 / jnp.maximum(norm0, 1.0)
        coef[1] = ratio0

        def second(i):
            tan = 1.5 - w_s[at(base, i), :]
            ratio = wide(1, i)
            acc = jnp.zeros((RC, NP), F32)
            for c in range(COMP):
                rows = at(c * BW, i)
                r = r1_s[rows, :]
                im = y_s[rows, :] + tan * r + ratio * im0_s[rows, :]
                y_s[rows, :] = im
                acc = acc + (r + ratio * r0_s[rows, :]) * im
            partial(3, i, acc)

        chunks(second)
        energy = total(3)
        size1 = norm1 / jnp.maximum(energy, 1.0)
        coef[2] = size1

        def second_step(i):
            size = wide(2, i)
            sq = jnp.zeros((RC, NP), F32)
            cross = jnp.zeros((RC, NP), F32)
            for c in range(COMP):
                rows = at(c * BW, i)
                im = y_s[rows, :]
                r = r1_s[rows, :] - size * im
                r2_s[rows, :] = r
                sq = sq + r * r
                cross = cross + r * im
            partial(4, i, sq)
            partial(5, i, cross)
            partial(6, i, (1.5 - w_s[at(base, i), :]) * sq)

        chunks(second_step)
        y_s[...] = product(r2_s, 2)
        norm2 = total(4)
        ratio1 = norm2 / jnp.maximum(norm1, 1.0)
        rest = total(6) + ratio1 * (2.0 * total(5) + ratio1 * energy)

        def third(i):
            acc = jnp.zeros((RC, NP), F32)
            for c in range(COMP):
                rows = at(c * BW, i)
                r = r2_s[rows, :]
                acc = acc + (2.0 * r - r.astype(BF).astype(F32)) * y_s[rows, :]
            partial(7, i, acc)

        chunks(third)
        a2 = norm2 / jnp.maximum(total(7) + rest, 1.0)
        a1 = size1 + a2 * ratio1
        coef[3] = size0 + a1 * ratio0
        coef[4] = a1
        coef[5] = a2

        def last(i):
            here = at(base, i)
            w = w_s[here, :]
            tan = 1.5 - w
            a = [wide(3 + k, i) for k in range(3)]
            flow = jnp.zeros((RC, NP), F32)
            for c in range(COMP):
                rows = at(c * BW, i)
                x = a[0] * r0_s[rows, :] + a[1] * r1_s[rows, :] + a[2] * r2_s[rows, :]
                flow = flow + prow[c, 0:RC, :] * x
                ycat[here, pl.ds(c * NP, NP)] = tan * x
            h_s[here, :] = h_s[here, :] + w * flow

        chunks(last)

        hi, lo = split2(h_s[pl.ds(pl.multiple_of(base, BW), BW), :])
        ucat[pl.ds(pl.multiple_of(2 * base, BW), BW), :] = hi
        ucat[pl.ds(pl.multiple_of(2 * base + BW, BW), BW), :] = lo

        for k in range(NBLK):
            j = NBLK - 1 - k

            @pl.when(b == k)
            def _():
                t8 = float(CAP) * iota((DEV, BW), 0) + 2.0 * j
                parts = []
                for n in range(k + 1):
                    srow = slotrow[0:1, n * BW : (n + 1) * BW]
                    one = jnp.concatenate(
                        [jnp.where(srow == t8, 1.0, 0.0), jnp.where(srow == t8 + 1.0, 1.0, 0.0)],
                        axis=0,
                    ).astype(BF)
                    parts += [one, one]
                moved = dot(jnp.concatenate(parts, axis=1), ucat[0 : 2 * (k + 1) * BW, :])
                ship[:, 2 * j, :] = moved[0:DEV]
                ship[:, 2 * j + 1, :] = moved[DEV:]
                if k == 0:
                    pl.semaphore_wait(column_sem, MACRO - 1)

                def send(i, c):
                    peer = lax.rem(me + i * STRIDE, DEV)
                    pltpu.make_async_remote_copy(
                        src_ref=ship.at[peer, pl.ds(2 * j, 2)],
                        dst_ref=recv.at[me, pl.ds(2 * j, 2)],
                        send_sem=send_sem.at[k],
                        recv_sem=recv_sem.at[k],
                        device_id=peer,
                        device_id_type=LOG,
                    ).start()
                    return c

                lax.fori_loop(1, DEV, send, 0, unroll=127)

        return carry

    lax.fori_loop(0, NBLK, block, 0)
    own = pltpu.make_async_copy(ship.at[me], recv.at[me], loc_sem)
    own.start()

    strain_p = dot_t(s32[...], servest[...])
    delta = jnp.zeros((8, RV), F32)
    for c in range(COMP):
        lanes = pl.ds(c * NP, NP)
        hi, lo = split2(ycat[:, lanes])
        with_hi = dot_t(gmat[:, lanes], hi)
        delta += with_hi[0:8] + with_hi[8:16] + dot_t(gmat[:, lanes], lo)[0:8]
    stress = strain_p[8:16] + strain_p[16:24] + strain_p[24:32]
    stress = stress + delta * (1.0 / math.sqrt(COMP * NODES))
    back = dot(stack(split3(stress)), servest[...])
    stress_ref[...] = (back[0:8] + back[8:16] + back[16:24])[0:VOIGT]
    own.wait()
    for k in range(NBLK):
        two_rows = pl.ds(2 * (NBLK - 1 - k), 2)
        some = pl.ds(0, DEV - 1)
        pltpu.make_async_copy(ship.at[some, two_rows], recv.at[some, two_rows], recv_sem.at[k]).wait()
        pltpu.make_async_copy(ship.at[some, two_rows], recv.at[some, two_rows], send_sem.at[k]).wait()


def turn(raw_ref, raw_stress_ref, out_hbm, stress_ref, buf, sem):
    stress_ref[...] = raw_stress_ref[...]
    copies = []
    for i in range(DEV * CAP // OUTW):
        for k in range(OUTW // BW):
            first = i * OUTW + k * BW
            piece = raw_ref[pl.ds(first // CAP, BW // CAP)].reshape(BW, NP)
            buf[:, pl.ds(first, BW)] = jnp.transpose(piece)[0:NODES]
        part = pl.ds(i * OUTW, OUTW)
        copies.append(pltpu.make_async_copy(buf.at[:, part], out_hbm.at[:, part], sem.at[i]))
        copies[i].start()
    for copy in copies:
        copy.wait()


def shards(
    history, yield_flags, strain, qp_to_rve, new_owner, stiffness, pattern, coupling, plastic_dir
):
    owner = new_owner.reshape(1, RV)
    hbm = pl.BlockSpec(memory_space=pl.ANY)
    vmem = pl.BlockSpec(memory_space=pltpu.VMEM)
    v = pltpu.VMEM
    raw, raw_stress = pl.pallas_call(
        kernel,
        out_shape=(
            v((DEV, CAP, NP), F32),
            v((VOIGT, RV), F32),
        ),
        in_specs=[hbm] * 6 + [pl.BlockSpec(memory_space=pltpu.SMEM)] + [hbm] * 2,
        out_specs=(vmem, vmem),
        scratch_shapes=[
            v((NODES, RV), F32), v((NODES, RV), jnp.int32), v((VOIGT, RV), F32),
            v((1, RV), jnp.int32), v((1, RV), jnp.int32), v((NB, NB, BLK, BLK), F32),
            v((COMP, VOIGT, NODES), F32), v((COMP, NODES), F32),
            v((NP, NP), F32), v((3 * NP, NP), BF), v((NP, 2 * RV), BF), v((NP, RV), BF),
            v((8, RV), F32), v((32, RV), BF), v((RV, 2 * RV), BF), v((RV, RV), BF),
            v((RV, COMP * NP), F32), v((COMP, 8, NP), F32), v((16, COMP * NP), BF),
            v((RV, NP), F32), v((RV, NP), F32),
            v((COMP * BW, NP), F32), v((COMP * BW, NP), F32), v((COMP * BW, NP), F32),
            v((COMP * BW, NP), F32), v((COMP * BW, NP), F32),
            v((RV, COMP * NP), F32), v((2 * RV, NP), BF), v((6, BW, 128), F32), v((8, BW, 128), F32),
            v((DEV, CAP, NP), F32),
            pltpu.SemaphoreType.DMA((20,)), pltpu.SemaphoreType.DMA(()),
            pltpu.SemaphoreType.DMA((NBLK,)), pltpu.SemaphoreType.DMA((NBLK,)),
            pltpu.SemaphoreType.REGULAR,
        ],
        compiler_params=pltpu.CompilerParams(
            collective_id=0, has_side_effects=True, vmem_limit_bytes=56 * 1024 * 1024
        ),
        name="micro_newton",
    )(
        history, yield_flags, strain, qp_to_rve, owner, stiffness, pattern, coupling, plastic_dir
    )
    return pl.pallas_call(
        turn,
        out_shape=(
            jax.ShapeDtypeStruct((NODES, DEV * CAP), F32),
            jax.ShapeDtypeStruct((VOIGT, RV), F32),
        ),
        in_specs=[vmem, vmem],
        out_specs=(hbm, vmem),
        scratch_shapes=[
            v((NODES, DEV * CAP), F32), pltpu.SemaphoreType.DMA((DEV * CAP // OUTW,)),
        ],
        compiler_params=pltpu.CompilerParams(vmem_limit_bytes=16 * 1024 * 1024),
        name="turn_history",
    )(raw, raw_stress)


def solution(mesh):
    both = ("macro", "pool")
    return jax.shard_map(
        shards,
        mesh=mesh,
        in_specs=(
            P(None, both), P(None, both), P(None, both), P(both, None), P(both, None),
            P(), P(), P(), P(),
        ),
        out_specs=(P(None, both), P(None, both)),
        check_vma=False,
    )
```
